128 devices in a mesh: feat: 32 (over z, y, core), cls: 4 (over x).
Axes of the slice: x: 4, y: 4, z: 4, core: 2. Of those that a mesh axis runs over, the one named last changes fastest.
Arguments:
- inputs: bfloat16 [2, 1024, 360], P(None, 'feat'), may hold values from -6 to 6
- projection: bfloat16 [360, 65536], P(None, 'feat'), may hold values from -0.3125 to 0.3125
- offsets: int32 [65536], P('feat'), may hold values from 0 to 65520
- labels: int32 [2, 1024], replicated, may hold values from 0 to 4999
- weights: float32 [65536, 5000], P('feat', 'cls'), may hold values from -6 to 6
Outputs:
- updated_weights: float32 [65536, 5000], P('feat', 'cls')
- losses: float32 [2], replicated
The draws below stay inside these ranges and needn't reach their ends.
All inputs are finite; a program needn't handle non-finite values.
Results may differ from the reference program's by a relative error of at most 0.00061.
Values may be sent and summed in bfloat16 or wider, within the bound.
A program may use at most 128 MiB of HBM per device.

```python
import math
import jax
import jax.numpy as jnp
from jax import lax

DIN = 360
NFEAT = 65536
NCLS = 5000
FRAMES = 1024
PANELS = 2


def place_ends(result, key, low, high):
    place = [jax.random.randint(jax.random.fold_in(key, axis), (), 0, length) for axis, length in enumerate(result.shape)]
    main_axis = result.shape.index(max(result.shape))
    next_to = place[:main_axis] + [(place[main_axis] + 1) % result.shape[main_axis]] + place[main_axis + 1:]
    return result.at[tuple(place)].set(low).at[tuple(next_to)].set(high)


def levels(stream_key, dims, shards, smallest, largest):
    gain = 1.0
    for dim, shards_of in shards:
        draws = jax.random.uniform(jax.random.fold_in(jax.random.fold_in(stream_key, 6), dim), (shards_of,), jnp.float32, smallest / len(shards), largest / len(shards))
        gain = gain * jnp.repeat(jnp.exp(draws), dims[dim] // shards_of).reshape((-1,) + (1,) * (len(dims) - 1 - dim))
    return gain


def centred(stream_key, extent, scale, reach, pieces=(), kind=jnp.bfloat16):
    level = levels(stream_key, extent, pieces, -0.22, 0.18) if pieces else 1.0
    array = jax.random.normal(stream_key, extent, jnp.float32) * scale * level
    return jnp.minimum(jnp.maximum(array, -reach), reach).astype(kind)


def setup_inputs(seed: int = 0) -> dict:
    keys = jax.random.split(jax.random.key(seed), 6)
    inputs = centred(keys[0], (PANELS, FRAMES, DIN), 1.0, 6.0, ((1, 32),))
    projection = centred(keys[1], (DIN, NFEAT), DIN ** -0.5, 0.3125, ((1, 32),))
    offsets = place_ends(jax.random.randint(keys[2], (NFEAT,), 0, 65521), jax.random.fold_in(keys[2], 1), 0, 65520).astype(jnp.int32)
    labels = place_ends(jax.random.randint(keys[3], (PANELS, FRAMES), 0, NCLS), jax.random.fold_in(keys[3], 1), 0, NCLS - 1).astype(jnp.int32)
    weights = centred(keys[4], (NFEAT, NCLS), 1.0, 6.0, ((0, 32), (1, 4)), jnp.float32)
    return {"inputs": inputs, "projection": projection, "offsets": offsets, "labels": labels, "weights": weights}


learning_rate = 10.0

def reference(inputs, projection, offsets, labels, weights):
    phase = offsets.astype(jnp.float32) * (2.0 * math.pi / 65521.0) - math.pi
    block = math.gcd(NFEAT, 4096)
    blocks = NFEAT // block
    classes = jnp.arange(NCLS, dtype=jnp.int32)
    feature_scale = math.sqrt(2.0 / NFEAT)
    losses = []
    for panel_index in range(PANELS):
        features = (feature_scale * jnp.cos(jnp.dot(inputs[panel_index], projection, preferred_element_type=jnp.float32) + phase)).astype(jnp.bfloat16)

        def add_block(running, index):
            start = (index * block).astype(jnp.int32)
            feature_block = lax.dynamic_slice_in_dim(features, start, block, 1)
            weight_block = lax.dynamic_slice_in_dim(weights, start, block, 0).astype(jnp.bfloat16)
            return (running + jnp.dot(feature_block, weight_block, preferred_element_type=jnp.float32), None)
        scores, _ = lax.scan(add_block, jnp.zeros((FRAMES, NCLS), jnp.float32), jnp.arange(blocks, dtype=jnp.int32))
        is_target = labels[panel_index][:, None] == classes[None, :]
        target = lax.optimization_barrier(jnp.sum(jnp.where(is_target, scores, 0.0), axis=1))
        margin = jnp.where(is_target, 0.0, jnp.maximum(0.0, 1.0 + scores - target[:, None]))
        slope = 2.0 * margin / (NCLS - 1)
        others = lax.optimization_barrier(jnp.sum(slope, axis=1))
        losses.append(jnp.sum(lax.optimization_barrier(jnp.sum(margin * margin, axis=1)) / (NCLS - 1)))
        step_grad = jnp.where(is_target, -others[:, None], slope).astype(jnp.bfloat16)

        def update(index):
            start = (index * block).astype(jnp.int32)
            feature_block = lax.dynamic_slice_in_dim(features, start, block, 1)
            weight_block = lax.dynamic_slice_in_dim(weights, start, block, 0)
            gradient = jnp.dot(feature_block.T, step_grad, preferred_element_type=jnp.float32)
            return weight_block - learning_rate * gradient
        weights = lax.map(update, jnp.arange(blocks, dtype=jnp.int32)).reshape(NFEAT, NCLS)
    return (weights, jnp.stack(losses))
```

```python
import math

import jax
import jax.numpy as jnp
from jax import lax
from jax.experimental import pallas as pl
from jax.experimental.pallas import tpu as pltpu
from jax.sharding import PartitionSpec as P

DIN, DPAD = 360, 384
NFEAT = 65536
NCLS = 5000
FRAMES = 1024
FEATS = 2048
CLS = 1250
CPAD = 1280
GRAM = 256
RATE = 10.0
MESH = pl.DeviceIdType.MESH
BF, F32 = jnp.bfloat16, jnp.float32
SINE = (6.2831851595779975, -41.34165492085313, 81.60099762206104, -76.54964291002278, 39.53570242669577)


def m4(v):
    return lax.rem(v, 4)


def step_kernel(
    inp, proj, off, lab, w_hbm,
    f1_hbm, g_hbm, wp_hbm,
    xb, pb, wf, wn, fb, ows, owk, ps, pr, psk, prk,
    s1_0, s1_1, r1_0, r1_1, s2_0, s2_1, r2_0, r2_1, own_0, own_1,
    so, sk, kg, tg, ox, lt, gb, ssem, rsem, lsem,
):
    feat, x = lax.axis_index("feat"), lax.axis_index("cls")
    c = lax.rem(feat, 2)
    y = m4(feat // 2)
    z = feat // 8
    p1 = y * (1 - c) + z * c
    p2 = z * (1 - c) + y * c

    def at(a, b):
        return ((b * (1 - c) + a * c) * 8 + (a * (1 - c) + b * c) * 2 + c, x)

    right1, left1 = at(m4(p1 + 1), p2), at(m4(p1 + 3), p2)
    right2, left2 = at(p1, m4(p2 + 1)), at(p1, m4(p2 + 3))
    partner = (feat + 1 - 2 * c, x)
    others_x = [(feat, m4(x + j)) for j in (1, 2, 3)]

    drain = []

    def rc(src, dst, i, dev):
        return pltpu.make_async_remote_copy(
            src_ref=src, dst_ref=dst, send_sem=ssem.at[i], recv_sem=rsem.at[i], device_id=dev, device_id_type=MESH
        )

    def send(ends, i, dev):
        rc(*ends(), i, dev).start()
        drain.append(lambda: rc(*ends(), i, dev).wait_send())

    def recv(region, i):
        rc(region, region, i, partner).wait_recv()

    counter = [0]

    def sems(n):
        counter[0] += n
        return counter[0] - n

    def rows_at(cc, b1, b2=0, extra=0, size=128):
        start = cc * 512 + b1 * 128 + b2 * 32 + extra
        return pl.ds(pl.multiple_of(start, min(size, 128)), size)

    w_in = [pltpu.make_async_copy(w_hbm.at[pl.ds(t * 256, 256)], wf.at[pl.ds(t * 256, 256)], lsem.at[t]) for t in range(8)]
    proj_in = pltpu.make_async_copy(proj, pb.at[pl.ds(0, DIN)], lsem.at[8])
    proj_in.start()
    for cp in w_in:
        cp.start()

    own = lambda: rows_at(c, p1, p2, 0, 32)
    for p in range(2):
        xb[p, own(), :] = jnp.zeros((32, DPAD), BF)
        xb[p, own(), 0:DIN] = inp[p]

    barrier = pltpu.get_barrier_semaphore()
    for dev in [right1, left1, right2, left2, partner] + others_x:
        pl.semaphore_signal(barrier, inc=1, device_id=dev, device_id_type=MESH)
    pl.semaphore_wait(barrier, 8)

    class Gather:
        def __init__(self, buf):
            self.buf = buf
            self.base = sems(12)

        def put(self, rows, i, dev):
            send(lambda: (self.buf().at[rows()], self.buf().at[rows()]), self.base + i, dev)

        def take(self, rows, i):
            recv(self.buf().at[rows()], self.base + i)

        def step0(self):
            self.put(own, 0, right2)
            self.put(own, 1, left2)

        def step1(self):
            self.take(lambda: rows_at(c, p1, m4(p2 + 3), 0, 32), 0)
            self.put(lambda: rows_at(c, p1, m4(p2 + 3), 0, 16), 2, right2)
            self.take(lambda: rows_at(c, p1, m4(p2 + 1), 0, 32), 1)
            self.put(lambda: rows_at(c, p1, m4(p2 + 1), 16, 16), 3, left2)

        def step2(self):
            self.take(lambda: rows_at(c, p1, m4(p2 + 2), 0, 16), 2)
            self.take(lambda: rows_at(c, p1, m4(p2 + 2), 16, 16), 3)
            blk = lambda: rows_at(c, p1)
            self.put(blk, 4, right1)
            self.put(blk, 5, left1)
            self.put(blk, 8, partner)

        def step3(self):
            self.take(lambda: rows_at(c, m4(p1 + 3)), 4)
            self.put(lambda: rows_at(c, m4(p1 + 3), 0, 0, 64), 6, right1)
            self.put(lambda: rows_at(c, m4(p1 + 3)), 9, partner)
            self.take(lambda: rows_at(c, m4(p1 + 1)), 5)
            self.put(lambda: rows_at(c, m4(p1 + 1), 0, 64, 64), 7, left1)
            self.put(lambda: rows_at(c, m4(p1 + 1)), 10, partner)

        def step4(self):
            self.take(lambda: rows_at(c, m4(p1 + 2), 0, 0, 64), 6)
            self.take(lambda: rows_at(c, m4(p1 + 2), 0, 64, 64), 7)
            self.put(lambda: rows_at(c, m4(p1 + 2)), 11, partner)

        def step5(self):
            for i, d in enumerate((0, 3, 1, 2)):
                self.take(lambda: rows_at(1 - c, m4(p2 + d)), 8 + i)

    gx = [Gather(lambda p=p: xb.at[p]) for p in range(2)]
    gg = [Gather(lambda p=p: gb.at[p]) for p in range(2)]

    gx[0].step0()
    gx[1].step0()

    pb[DIN:DPAD, :] = jnp.zeros((DPAD - DIN, FEATS), BF)
    turns = off[...].astype(F32) * F32(1.0 / 65521.0)
    lab_col = pl.multiple_of((feat // 4) * 128, 128)
    for p in range(2):
        row = lab[pl.ds(p, 1), pl.ds(lab_col, 128)].astype(F32)
        lt[p] = jnp.broadcast_to(row, (128, 128)).T
    gx[0].step1()
    gx[1].step1()
    wn[:, 1152:CPAD] = jnp.zeros((FEATS, CPAD - 1152), BF)

    def narrow(t):
        w_in[t].wait()
        wn[pl.ds(t * 256, 256), 0:CLS] = wf[pl.ds(t * 256, 256), :].astype(BF)

    narrow(0)
    gx[0].step2()
    gx[1].step2()
    narrow(1)
    narrow(2)
    gx[0].step3()
    narrow(3)
    narrow(4)
    gx[0].step4()
    gx[1].step3()
    narrow(5)
    narrow(6)
    narrow(7)
    proj_in.wait()
    gx[0].step5()

    scale = math.sqrt(2.0 / NFEAT)
    coef = [F32(v * scale) for v in SINE]

    def features(p, rows):
        acc = jnp.dot(xb[p, rows, :], pb[...], preferred_element_type=F32)
        u = acc * F32(1.0 / (2.0 * math.pi)) + turns
        q = jnp.abs(u - jnp.round(u)) - 0.25
        q2 = q * q
        r = coef[4]
        for v in coef[3::-1]:
            r = r * q2 + v
        fb[p, rows, :] = (r * q).astype(BF)

    def scores(p, rows):
        return jnp.dot(fb[p, rows, :], wn[...], preferred_element_type=F32)

    def gram(rows):
        quarter = pl.ds(pl.multiple_of(x * GRAM, GRAM), GRAM)
        return lax.dot_general(
            fb[1, rows, :], fb[0, quarter, :], (((1,), (1,)), ((), ())), preferred_element_type=F32
        )

    S1, R1, S2, R2, OWN = (s1_0, s1_1), (r1_0, r1_1), (s2_0, s2_1), (r2_0, r2_1), (own_0, own_1)
    pair_sem = sems(12)
    ring_sem = [sems(8), sems(8)]
    tg_sem, ox_sem, kg_sem = [sems(3), sems(3)], [sems(3), sems(3)], sems(3)

    def pair_recv(p, k):
        recv(pr.at[4 * p + k], pair_sem + 4 * p + k)
        if p:
            recv(prk.at[k], pair_sem + 8 + k)

    def combine(p, k, put, lo, hi):
        def body(i, _):
            rows = pl.ds(pl.multiple_of(i * 32, 32), 32)
            put(rows, slice(0, CPAD), ows[k, rows, :] + pr[4 * p + k, rows, :].astype(F32))
            if p:
                put(rows, slice(CPAD, CPAD + GRAM), owk[k, rows, :] + prk[k, rows, :].astype(F32))
            return 0

        lax.fori_loop(lo, hi, body, 0)

    def reduce0(p):
        pair_recv(p, 0)
        s, r, i = S1[p], R1[p], ring_sem[p]

        def put(rows, cols, v):
            s[0, rows, cols] = v.astype(BF)

        combine(p, 0, put, 0, 4)
        send(lambda: (s.at[0, pl.ds(0, 64)], r.at[pl.ds(0, 64)]), i, right1)
        send(lambda: (s.at[0, pl.ds(64, 64)], r.at[pl.ds(64, 64)]), i + 1, left1)

    def reduce1(p):
        pair_recv(p, 1)
        s, r, i = S1[p], R1[p], ring_sem[p]
        recv(r.at[pl.ds(0, 64)], i)

        def put_in(rows, cols, v):
            s[1, rows, cols] = (v + r[rows, cols].astype(F32)).astype(BF)

        def put(rows, cols, v):
            s[1, rows, cols] = v.astype(BF)

        combine(p, 1, put_in, 0, 2)
        combine(p, 1, put, 2, 4)
        send(lambda: (s.at[1], r.at[pl.ds(128, 128)]), i + 2, right1)

    def reduce2(p):
        pair_recv(p, 2)
        s, r, i = S1[p], R1[p], ring_sem[p]
        recv(r.at[pl.ds(64, 64)], i + 1)

        def put_in(rows, cols, v):
            s[2, rows, cols] = (v + r[rows, cols].astype(F32)).astype(BF)

        def put(rows, cols, v):
            s[2, rows, cols] = v.astype(BF)

        combine(p, 2, put, 0, 2)
        combine(p, 2, put_in, 2, 4)
        send(lambda: (s.at[2], r.at[pl.ds(256, 128)]), i + 3, left1)

    def sub(d, extra=0, size=32):
        return pl.ds(pl.multiple_of(m4(p2 + d) * 32 + extra, 16), size)

    def reduce3(p):
        pair_recv(p, 3)
        r, i, o = R1[p], ring_sem[p], OWN[p]
        recv(r.at[pl.ds(128, 128)], i + 2)
        recv(r.at[pl.ds(256, 128)], i + 3)

        def put(rows, cols, v):
            a = pl.ds(pl.multiple_of(rows.start + 128, 32), 32)
            b = pl.ds(pl.multiple_of(rows.start + 256, 32), 32)
            o[rows, cols] = v + r[a, cols].astype(F32) + r[b, cols].astype(F32)

        combine(p, 3, put, 0, 4)
        s, r = S2[p], R2[p]
        s[pl.ds(0, 32), :] = o[sub(2), :].astype(BF)
        send(lambda: (s.at[pl.ds(0, 16)], r.at[pl.ds(0, 16)]), i + 4, right2)
        send(lambda: (s.at[pl.ds(16, 16)], r.at[pl.ds(16, 16)]), i + 5, left2)

    def reduce4(p):
        s, r, i, o = S2[p], R2[p], ring_sem[p], OWN[p]
        recv(r.at[pl.ds(0, 16)], i + 4)
        s[pl.ds(32, 16), :] = (o[sub(1, 0, 16), :] + r[pl.ds(0, 16), :].astype(F32)).astype(BF)
        s[pl.ds(48, 16), :] = o[sub(1, 16, 16), :].astype(BF)
        send(lambda: (s.at[pl.ds(32, 32)], r.at[pl.ds(32, 32)]), i + 6, right2)
        recv(r.at[pl.ds(16, 16)], i + 5)
        s[pl.ds(64, 16), :] = o[sub(3, 0, 16), :].astype(BF)
        s[pl.ds(80, 16), :] = (o[sub(3, 16, 16), :] + r[pl.ds(16, 16), :].astype(F32)).astype(BF)
        send(lambda: (s.at[pl.ds(64, 32)], r.at[pl.ds(64, 32)]), i + 7, left2)

    def x_send(ref, base):
        for j in range(3):
            send(lambda: (ref().at[x], ref().at[x]), base + j, others_x[j])

    def x_recv(ref, base):
        for j in range(3):
            recv(ref().at[m4(x + 3 - j)], base + j)

    def reduce5(p):
        r, i, o = R2[p], ring_sem[p], OWN[p]
        recv(r.at[pl.ds(32, 32)], i + 6)
        recv(r.at[pl.ds(64, 32)], i + 7)
        total = o[sub(0), :] + r[pl.ds(32, 32), :].astype(F32) + r[pl.ds(64, 32), :].astype(F32)
        so[p] = total[:, 0:CPAD]
        if p:
            k12 = total[:, CPAD:]
            high = k12.astype(BF)
            kg[x, 0:32, :] = high
            kg[x, 32:64, :] = (k12 - high.astype(F32)).astype(BF)
            x_send(lambda: kg, kg_sem)

    lab_rows = pl.ds(pl.multiple_of(m4(feat) * 32, 32), 32)
    col = lax.broadcasted_iota(jnp.int32, (32, CPAD), 1)
    lane = lax.broadcasted_iota(jnp.int32, (32, 128), 1)

    def is_target(p):
        label = lt[p, lab_rows, 0:1].astype(jnp.int32) - x * CLS
        return (col == label) & (col < CLS)

    def find_target(p):
        if p:
            x_recv(lambda: kg, kg_sem)
            moved = jnp.zeros((64, CPAD), F32)
            for j in range(4):
                moved += jnp.dot(kg[j], gb[0, j * GRAM:(j + 1) * GRAM, :], preferred_element_type=F32)
            so[p] = so[p] - RATE * (moved[0:32] + moved[32:64])
        part = jnp.sum(jnp.where(is_target(p), so[p], 0.0), axis=1, keepdims=True)
        tg[p, x] = jnp.broadcast_to(part, (32, 128))
        x_send(lambda: tg.at[p], tg_sem[p])

    def find_margin(p):
        x_recv(lambda: tg.at[p], tg_sem[p])
        target = (tg[p, 0] + tg[p, 1] + tg[p, 2] + tg[p, 3])[:, 0:1]
        keep = (col < CLS) & jnp.logical_not(is_target(p))
        margin = jnp.where(keep, jnp.maximum(0.0, 1.0 + so[p] - target), 0.0)
        slope = margin * F32(2.0 / (NCLS - 1))
        so[p] = slope
        out = jnp.sum(slope, axis=1, keepdims=True)
        loss = jnp.sum(margin * margin, axis=1, keepdims=True) * F32(1.0 / (NCLS - 1))
        ox[p, x] = jnp.where(lane < 64, out, loss)
        x_send(lambda: ox.at[p], ox_sem[p])

    def find_grad(p):
        x_recv(lambda: ox.at[p], ox_sem[p])
        both = ox[p, 0] + ox[p, 1] + ox[p, 2] + ox[p, 3]
        out, loss = both[:, 0:1], both[:, 64:65]
        high = loss.astype(BF).astype(F32)
        mid = (loss - high).astype(BF).astype(F32)
        low = loss - high - mid
        g = jnp.where(is_target(p), -out, so[p])
        g = jnp.where(col == CLS, high, g)
        g = jnp.where(col == CLS + 1, mid, g)
        g = jnp.where(col == CLS + 2, low, g)
        gb[p, own(), :] = g.astype(BF)
        gg[p].step0()

    before = {
        1: [lambda: reduce0(0)],
        2: [lambda: reduce1(0)],
        3: [lambda: reduce2(0)],
        4: [lambda: reduce3(0)],
        5: [lambda: reduce5(0), lambda: find_target(0), lambda: reduce0(1)],
        6: [lambda: find_grad(0), lambda: reduce1(1)],
        7: [lambda: gg[0].step2(), lambda: reduce2(1)],
    }
    after = {
        1: [lambda: gx[1].step4()],
        2: [lambda: gx[1].step5()],
        4: [lambda: reduce4(0)],
        5: [lambda: find_margin(0)],
        6: [lambda: gg[0].step1()],
        7: [lambda: gg[0].step3()],
    }

    def run(tasks, s):
        for at_step, fns in tasks.items():

            @pl.when(s == at_step)
            def _(fns=fns):
                for fn in fns:
                    fn()

    def panel_step(s, _):
        p, k = s // 4, lax.rem(s, 4)
        d = 2 - k + 3 * (k // 2) - 2 * (k // 3)
        theirs = rows_at(1 - c, m4(p2 + d))
        mine = rows_at(c, m4(p1 + d))

        def feat_body(j, _):
            half = (1 - c) * (1 - j) + c * j
            blk = m4(p2 + d) * (1 - j) + m4(p1 + d) * j
            features(p, rows_at(half, blk))
            return 0

        lax.fori_loop(0, 2, feat_body, 0)
        run(before, s)
        ps[s] = scores(p, theirs).astype(BF)
        rc(ps.at[s], pr.at[s], pair_sem + s, partner).start()

        @pl.when(s >= 4)
        def _():
            psk[k] = gram(theirs).astype(BF)
            rc(psk.at[k], prk.at[k], pair_sem + 8 + k, partner).start()
            owk[k] = gram(mine)

        ows[k] = scores(p, mine)
        run(after, s)
        return 0

    lax.fori_loop(0, 8, panel_step, 0)
    for k in range(8):
        drain.append(lambda k=k: rc(ps.at[k], pr.at[k], pair_sem + k, partner).wait_send())
    for k in range(4):
        drain.append(lambda k=k: rc(psk.at[k], prk.at[k], pair_sem + 8 + k, partner).wait_send())

    f1_out = pltpu.make_async_copy(fb.at[1], f1_hbm, lsem.at[9])
    f1_out.start()
    reduce3(1)
    gg[0].step4()
    reduce4(1)
    gg[0].step5()
    reduce5(1)

    def wp_out(t):
        rows = pl.ds(pl.multiple_of(t * 256, 256), 256)
        return pltpu.make_async_copy(wf.at[rows], wp_hbm.at[rows], lsem.at[10])

    tail = {
        0: [lambda: find_target(1)],
        1: [lambda: find_margin(1)],
        2: [lambda: find_grad(1)],
        3: [lambda: gg[1].step1()],
        4: [lambda: gg[1].step2()],
        5: [lambda: gg[1].step3()],
        6: [lambda: gg[1].step4()],
        7: [lambda: gg[1].step5()],
    }

    def update_step(t, _):
        rows = pl.ds(pl.multiple_of(t * 256, 256), 256)
        gradient = lax.dot_general(
            fb[0, :, rows], gb[0], (((0,), (0,)), ((), ())), preferred_element_type=F32
        )
        wf[rows, :] = wf[rows, :] - RATE * gradient[:, 0:CLS]
        run(tail, t)
        return 0

    lax.fori_loop(0, 8, update_step, 0)
    wp_copy = pltpu.make_async_copy(wf, wp_hbm, lsem.at[10])
    wp_copy.start()
    g_out = pltpu.make_async_copy(gb, g_hbm, lsem.at[11])
    g_out.start()
    for fn in drain:
        fn()
    f1_out.wait()
    wp_copy.wait()
    g_out.wait()


def last_kernel(w, f, g, l0, l1, out, loss):
    gradient = lax.dot_general(f[...], g[0], (((0,), (0,)), ((), ())), preferred_element_type=F32)
    out[...] = w[...] - RATE * gradient[:, 0:CLS]

    @pl.when(pl.program_id(0) == 0)
    def _():
        lane = lax.broadcasted_iota(jnp.int32, (FRAMES, 128), 1)
        first = CLS - 1152
        here = (lane >= first) & (lane < first + 3)
        for p, ref in ((0, l0), (1, l1)):
            total = jnp.sum(jnp.where(here, ref[0].astype(F32), 0.0), axis=0, keepdims=True)
            total = jnp.sum(total, axis=1, keepdims=True)
            loss[pl.ds(p, 1), :] = jnp.broadcast_to(total, (1, 128))


def per_device(inputs, projection, offsets, labels, weights):
    vm = pl.BlockSpec(memory_space=pltpu.VMEM)
    hbm = pl.BlockSpec(memory_space=pl.ANY)
    v = pltpu.VMEM
    wide = (CPAD, CPAD + GRAM)
    f1, g, wp = pl.pallas_call(
        step_kernel,
        out_shape=(
            jax.ShapeDtypeStruct((FRAMES, FEATS), BF),
            jax.ShapeDtypeStruct((2, FRAMES, CPAD), BF),
            jax.ShapeDtypeStruct((FEATS, CLS), F32),
        ),
        in_specs=[vm, hbm, vm, vm, hbm],
        out_specs=(hbm, hbm, hbm),
        scratch_shapes=[
            v((2, FRAMES, DPAD), BF), v((DPAD, FEATS), BF), v((FEATS, CLS), F32), v((FEATS, CPAD), BF),
            v((2, FRAMES, FEATS), BF), v((4, 128, CPAD), F32), v((4, 128, GRAM), F32),
            v((8, 128, CPAD), BF), v((8, 128, CPAD), BF), v((4, 128, GRAM), BF), v((4, 128, GRAM), BF),
            *[v((3, 128, w), BF) for w in wide], *[v((384, w), BF) for w in wide],
            *[v((96, w), BF) for w in wide], *[v((96, w), BF) for w in wide],
            *[v((128, w), F32) for w in wide],
            v((2, 32, CPAD), F32), v((32, GRAM), F32), v((4, 64, GRAM), BF),
            v((2, 4, 32, 128), F32), v((2, 4, 32, 128), F32), v((2, 128, 128), F32),
            v((2, FRAMES, CPAD), BF),
            pltpu.SemaphoreType.DMA((96,)), pltpu.SemaphoreType.DMA((96,)), pltpu.SemaphoreType.DMA((12,)),
        ],
        compiler_params=pltpu.CompilerParams(collective_id=0, has_side_effects=True, vmem_limit_bytes=65 * 1000 * 1000),
        name="panels",
    )(inputs, projection, offsets.reshape(1, FEATS), labels, weights)
    new, loss = pl.pallas_call(
        last_kernel,
        grid=(8,),
        out_shape=(jax.ShapeDtypeStruct((FEATS, CLS), F32), jax.ShapeDtypeStruct((2, 128), F32)),
        in_specs=[
            pl.BlockSpec((256, CLS), lambda i: (i, 0)),
            pl.BlockSpec((FRAMES, 256), lambda i: (0, i)),
            pl.BlockSpec((1, FRAMES, CPAD), lambda i: (1, 0, 0)),
            pl.BlockSpec((1, FRAMES, 128), lambda i: (0, 0, 9)),
            pl.BlockSpec((1, FRAMES, 128), lambda i: (1, 0, 9)),
        ],
        out_specs=(pl.BlockSpec((256, CLS), lambda i: (i, 0)), pl.BlockSpec((2, 128), lambda i: (0, 0))),
        compiler_params=pltpu.CompilerParams(vmem_limit_bytes=48 * 2**20),
        name="last_update",
    )(wp, f1, g, g, g)
    return new, loss[:, 0]


def solution(mesh):
    return jax.shard_map(
        per_device,
        mesh=mesh,
        in_specs=(P(None, "feat", None), P(None, "feat"), P("feat"), P(), P("feat", "cls")),
        out_specs=(P("feat", "cls"), P()),
        check_vma=False,
    )
```

```python
import math

import jax
import jax.numpy as jnp
from jax import lax
from jax.experimental import pallas as pl
from jax.experimental.pallas import tpu as pltpu
from jax.sharding import PartitionSpec as P

DIN, DPAD = 360, 384
NFEAT = 65536
NCLS = 5000
FRAMES = 1024
FEATS = 2048
CLS = 1250
CPAD = 1280
GRAM = 256
TILES = 10
LAST = 1152
SEMS = 192
WIDE = (CPAD, CPAD + GRAM)
RATE = 10.0
MESH = pl.DeviceIdType.MESH
BF, F32 = jnp.bfloat16, jnp.float32
SINE = (6.2831851595779975, -41.34165492085313, 81.60099762206104, -76.54964291002278, 39.53570242669577)


def m4(v):
    return lax.rem(v, 4)


def step_kernel(
    inp, proj, off, lab, w_hbm,
    f1_hbm, g_hbm, wp_hbm,
    xb, pb, wf, tail_rows, wn, fb, ows, ps, pr,
    s1_0, s1_1, r1_0, r1_1, s2_0, s2_1, r2_0, r2_1, own_0, own_1,
    so, kg, tg, ox, lt, gb, ssem, rsem, lsem,
):
    feat, x = lax.axis_index("feat"), lax.axis_index("cls")
    c = lax.rem(feat, 2)
    y = m4(feat // 2)
    z = feat // 8
    p1 = y * (1 - c) + z * c
    p2 = z * (1 - c) + y * c

    def at(a, b):
        return ((b * (1 - c) + a * c) * 8 + (a * (1 - c) + b * c) * 2 + c, x)

    right1, left1 = at(m4(p1 + 1), p2), at(m4(p1 + 3), p2)
    across1 = at(m4(p1 + 2), p2)
    ring2 = [at(p1, m4(p2 + d)) for d in (1, 2, 3)]
    partner = (feat + 1 - 2 * c, x)
    others_x = [(feat, m4(x + j)) for j in (1, 2, 3)]

    drain = []

    def rc(src, dst, i, dev, j=None):
        return pltpu.make_async_remote_copy(
            src_ref=src,
            dst_ref=dst,
            send_sem=ssem.at[i],
            recv_sem=rsem.at[i if j is None else j],
            device_id=dev,
            device_id_type=MESH,
        )

    def send(ends, i, dev, j=None):
        rc(*ends(), i, dev, j).start()
        drain.append(lambda: rc(*ends(), i, dev, j).wait_send())

    def recv(region, i):
        rc(region, region, i, partner).wait_recv()

    counter = [0]

    def sems(n):
        counter[0] += n
        return counter[0] - n

    def rows_at(cc, b1, b2=0, extra=0, size=128):
        start = cc * 512 + b1 * 128 + b2 * 32 + extra
        return pl.ds(pl.multiple_of(start, min(size, 128)), size)

    w_in = pltpu.make_async_copy(w_hbm, wf, lsem.at[4])
    proj_in = pltpu.make_async_copy(proj, pb.at[pl.ds(0, DIN)], lsem.at[0])
    proj_in.start()
    w_in.start()
    tail_rows[...] = jnp.zeros((128, FEATS), F32)

    own = lambda: rows_at(c, p1, p2, 0, 32)
    for p in range(2):
        xb[p, own(), :] = jnp.zeros((32, DPAD), BF)
        xb[p, own(), 0:DIN] = inp[p]

    barrier = pltpu.get_barrier_semaphore()
    for dev in [right1, left1, across1, partner] + ring2 + others_x:
        pl.semaphore_signal(barrier, inc=1, device_id=dev, device_id_type=MESH)
    pl.semaphore_wait(barrier, 10)

    class Gather:
        def __init__(self, buf, direct):
            self.buf, self.direct = buf, direct
            self.base = sems(36)
            self.sent = 0

        def put(self, rows, i, dev):
            send(lambda: (self.buf().at[rows()], self.buf().at[rows()]), self.base + i, dev)

        def take(self, rows, i):
            recv(self.buf().at[rows()], self.base + i)

        def pass_on(self, rows):
            i = self.base + 23 + self.sent
            self.sent += 1
            send(lambda: (self.buf().at[rows()], self.buf().at[rows()]), i, partner, self.base + 23)

        def out1(self, j):
            rows = lambda: rows_at(c, p1, m4(p2 + j), 0, 32)
            self.put(rows, 3 + 3 * j, right1)
            self.put(rows, 5 + 3 * j, left1)
            if self.direct:
                self.put(rows, 4 + 3 * j, across1)
            self.pass_on(rows)

        def in1(self, j):
            b2 = m4(p2 + j)
            self.take(lambda: rows_at(c, m4(p1 + 3), b2, 0, 32), 3 + 3 * j)
            if not self.direct:
                self.put(lambda: rows_at(c, m4(p1 + 3), m4(p2 + j), 0, 16), 15 + 2 * j, right1)
            self.pass_on(lambda: rows_at(c, m4(p1 + 3), m4(p2 + j), 0, 32))
            self.take(lambda: rows_at(c, m4(p1 + 1), b2, 0, 32), 5 + 3 * j)
            if not self.direct:
                self.put(lambda: rows_at(c, m4(p1 + 1), m4(p2 + j), 16, 16), 16 + 2 * j, left1)
            self.pass_on(lambda: rows_at(c, m4(p1 + 1), m4(p2 + j), 0, 32))

        def step0(self):
            for d in (2, 1, 3):
                self.put(own, d - 1, ring2[d - 1])
            self.out1(0)

        def step1(self):
            for d in (1, 3, 2):
                self.take(lambda: rows_at(c, p1, m4(p2 + 4 - d), 0, 32), d - 1)
                self.out1(4 - d)

        def step2(self):
            self.in1(0)

        def step3(self):
            for j in (3, 1, 2):
                self.in1(j)

        def step4(self):
            for j in range(4):
                b2 = m4(p2 + j)
                if self.direct:
                    self.take(lambda: rows_at(c, m4(p1 + 2), b2, 0, 32), 4 + 3 * j)
                else:
                    self.take(lambda: rows_at(c, m4(p1 + 2), b2, 0, 16), 15 + 2 * j)
                    self.take(lambda: rows_at(c, m4(p1 + 2), b2, 16, 16), 16 + 2 * j)
            self.pass_on(lambda: rows_at(c, m4(p1 + 2)))

        def step5(self):
            self.take(lambda: rows_at(1 - c, 0, 0, 0, 512), 23)

    gx = [Gather(lambda p=p: xb.at[p], True) for p in range(2)]
    gg = [Gather(lambda p=p: gb.at[p], False) for p in range(2)]

    gx[0].step0()

    pb[DIN:DPAD, :] = jnp.zeros((DPAD - DIN, FEATS), BF)
    turns = off[...].astype(F32) * F32(1.0 / 65521.0)
    lab_col = pl.multiple_of((feat // 4) * 128, 128)
    for p in range(2):
        row = lab[pl.ds(p, 1), pl.ds(lab_col, 128)].astype(F32)
        lt[p] = jnp.broadcast_to(row, (128, 128)).T
    def narrow(t):
        if t < TILES - 1:
            rows = wf[pl.ds(t * 128, 128), :]
        else:
            tail_rows[0:CLS - LAST, :] = wf[LAST:CLS, :]
            rows = tail_rows[...]
        wn[:, t * 128:t * 128 + 128] = rows.astype(BF).T

    w_in.wait()
    for t in range(5):
        narrow(t)
    gx[0].step1()
    gx[1].step0()
    for t in range(5, 8):
        narrow(t)
    gx[0].step2()
    gx[0].step3()
    gx[0].step4()
    for t in range(8, TILES):
        narrow(t)
    gx[1].step1()
    proj_in.wait()
    gx[0].step5()

    scale = math.sqrt(2.0 / NFEAT)
    coef = [F32(v * scale) for v in SINE]

    def features(p, rows):
        acc = jnp.dot(xb[p, rows, :], pb[...], preferred_element_type=F32)
        u = acc * F32(1.0 / (2.0 * math.pi)) + turns
        q = jnp.abs(u - jnp.round(u)) - 0.25
        q2 = q * q
        r = coef[4]
        for v in coef[3::-1]:
            r = r * q2 + v
        fb[p, rows, :] = (r * q).astype(BF)

    def scores(p, rows):
        return jnp.dot(fb[p, rows, :], wn[:, 0:WIDE[p]], preferred_element_type=F32)

    S1, R1, S2, R2, OWN = (s1_0, s1_1), (r1_0, r1_1), (s2_0, s2_1), (r2_0, r2_1), (own_0, own_1)
    pair_sem = sems(8)
    ring_sem = [sems(8), sems(8)]
    tg_sem, ox_sem, kg_sem = [sems(3), sems(3)], [sems(3), sems(3)], sems(3)

    def pair_recv(p, k):
        recv(pr.at[4 * p + k, :, pl.ds(0, WIDE[p])], pair_sem + 4 * p + k)

    def combine(p, k, put, lo, hi):
        def body(i, _):
            rows = pl.ds(pl.multiple_of(i * 32, 32), 32)
            put(rows, slice(0, WIDE[p]), ows[k, rows, 0:WIDE[p]] + pr[4 * p + k, rows, 0:WIDE[p]].astype(F32))
            return 0

        lax.fori_loop(lo, hi, body, 0)

    def reduce0(p):
        pair_recv(p, 0)
        s, r, i = S1[p], R1[p], ring_sem[p]

        def put(rows, cols, v):
            s[0, rows, cols] = v.astype(BF)

        combine(p, 0, put, 0, 4)
        send(lambda: (s.at[0, pl.ds(0, 64)], r.at[pl.ds(0, 64)]), i, right1)
        send(lambda: (s.at[0, pl.ds(64, 64)], r.at[pl.ds(64, 64)]), i + 1, left1)

    def reduce1(p):
        pair_recv(p, 1)
        s, r, i = S1[p], R1[p], ring_sem[p]
        recv(r.at[pl.ds(0, 64)], i)

        def put_in(rows, cols, v):
            s[1, rows, cols] = (v + r[rows, cols].astype(F32)).astype(BF)

        def put(rows, cols, v):
            s[1, rows, cols] = v.astype(BF)

        combine(p, 1, put_in, 0, 2)
        combine(p, 1, put, 2, 4)
        send(lambda: (s.at[1], r.at[pl.ds(128, 128)]), i + 2, right1)

    def reduce2(p):
        pair_recv(p, 2)
        s, r, i = S1[p], R1[p], ring_sem[p]
        recv(r.at[pl.ds(64, 64)], i + 1)

        def put_in(rows, cols, v):
            s[2, rows, cols] = (v + r[rows, cols].astype(F32)).astype(BF)

        def put(rows, cols, v):
            s[2, rows, cols] = v.astype(BF)

        combine(p, 2, put, 0, 2)
        combine(p, 2, put_in, 2, 4)
        send(lambda: (s.at[2], r.at[pl.ds(256, 128)]), i + 3, left1)

    def sub(d, extra=0, size=32):
        return pl.ds(pl.multiple_of(m4(p2 + d) * 32 + extra, 16), size)

    def reduce3(p):
        pair_recv(p, 3)
        r, i, o = R1[p], ring_sem[p], OWN[p]
        recv(r.at[pl.ds(128, 128)], i + 2)
        recv(r.at[pl.ds(256, 128)], i + 3)

        def put(rows, cols, v):
            a = pl.ds(pl.multiple_of(rows.start + 128, 32), 32)
            b = pl.ds(pl.multiple_of(rows.start + 256, 32), 32)
            o[rows, cols] = v + r[a, cols].astype(F32) + r[b, cols].astype(F32)

        combine(p, 3, put, 0, 4)
        s, r = S2[p], R2[p]
        for d in (2, 1, 3):
            piece = pl.ds(32 * d - 32, 32)
            s[piece, :] = o[sub(d), :].astype(BF)
            send(lambda piece=piece: (s.at[piece], r.at[piece]), i + 3 + d, ring2[d - 1])

    def x_send(ref, base):
        for j in range(3):
            send(lambda: (ref().at[x], ref().at[x]), base + j, others_x[j])

    def x_recv(ref, base):
        for j in range(3):
            recv(ref().at[m4(x + 3 - j)], base + j)

    def reduce5(p):
        r, i, o = R2[p], ring_sem[p], OWN[p]
        total = o[sub(0), :]
        for d in (1, 3, 2):
            piece = pl.ds(32 * d - 32, 32)
            recv(r.at[piece], i + 3 + d)
            total += r[piece, :].astype(F32)
        so[p] = total[:, 0:CPAD]
        if p:
            k12 = total[:, CPAD:]
            high = k12.astype(BF)
            kg[x, 0:32, :] = high
            kg[x, 32:64, :] = (k12 - high.astype(F32)).astype(BF)
            x_send(lambda: kg, kg_sem)

    lab_rows = pl.ds(pl.multiple_of(m4(feat) * 32, 32), 32)
    col = lax.broadcasted_iota(jnp.int32, (32, CPAD), 1)
    lane = lax.broadcasted_iota(jnp.int32, (32, 128), 1)

    def is_target(p):
        label = lt[p, lab_rows, 0:1].astype(jnp.int32) - x * CLS
        return (col == label) & (col < CLS)

    def find_target(p):
        if p:
            x_recv(lambda: kg, kg_sem)
            moved = jnp.zeros((64, CPAD), F32)
            for j in range(4):
                moved += jnp.dot(kg[j], gb[0, j * GRAM:(j + 1) * GRAM, :], preferred_element_type=F32)
            so[p] = so[p] - RATE * (moved[0:32] + moved[32:64])
        part = jnp.sum(jnp.where(is_target(p), so[p], 0.0), axis=1, keepdims=True)
        tg[p, x] = jnp.broadcast_to(part, (32, 128))
        x_send(lambda: tg.at[p], tg_sem[p])

    def find_margin(p):
        x_recv(lambda: tg.at[p], tg_sem[p])
        target = (tg[p, 0] + tg[p, 1] + tg[p, 2] + tg[p, 3])[:, 0:1]
        keep = (col < CLS) & jnp.logical_not(is_target(p))
        margin = jnp.where(keep, jnp.maximum(0.0, 1.0 + so[p] - target), 0.0)
        slope = margin * F32(2.0 / (NCLS - 1))
        so[p] = slope
        out = jnp.sum(slope, axis=1, keepdims=True)
        loss = jnp.sum(margin * margin, axis=1, keepdims=True) * F32(1.0 / (NCLS - 1))
        ox[p, x] = jnp.where(lane < 64, out, loss)
        x_send(lambda: ox.at[p], ox_sem[p])

    def find_grad(p):
        x_recv(lambda: ox.at[p], ox_sem[p])
        both = ox[p, 0] + ox[p, 1] + ox[p, 2] + ox[p, 3]
        out, loss = both[:, 0:1], both[:, 64:65]
        high = loss.astype(BF).astype(F32)
        mid = (loss - high).astype(BF).astype(F32)
        low = loss - high - mid
        g = jnp.where(is_target(p), -out, so[p])
        g = jnp.where(col == CLS, high, g)
        g = jnp.where(col == CLS + 1, mid, g)
        g = jnp.where(col == CLS + 2, low, g)
        gb[p, own(), :] = g.astype(BF)
        gg[p].step0()

    before = {
        1: [lambda: reduce0(0)],
        2: [lambda: reduce1(0)],
        3: [lambda: reduce2(0)],
        4: [lambda: reduce3(0)],
        5: [lambda: reduce5(0), lambda: find_target(0), lambda: reduce0(1)],
        6: [lambda: find_grad(0), lambda: reduce1(1)],
        7: [lambda: gg[0].step1(), lambda: reduce2(1)],
    }
    between = {
        0: [lambda: gx[1].step2()],
        1: [lambda: gx[1].step3()],
        2: [lambda: gx[1].step4()],
        3: [lambda: gx[1].step5()],
        7: [lambda: gg[0].step2()],
    }
    after = {
        5: [lambda: find_margin(0)],
    }

    def run(tasks, s, panel=None):
        for at_step, fns in tasks.items():
            if panel is not None and at_step // 4 != panel:
                continue

            @pl.when(s == at_step)
            def _(fns=fns):
                for fn in fns:
                    fn()

    def panel_step(s, _):
        p, k = s // 4, lax.rem(s, 4)
        d = 2 - k + 3 * (k // 2) - 2 * (k // 3)
        theirs = rows_at(1 - c, m4(p2 + d))
        mine = rows_at(c, m4(p1 + d))

        def feat_body(j, _):
            half = (1 - c) * (1 - j) + c * j
            blk = m4(p2 + d) * (1 - j) + m4(p1 + d) * j
            features(p, rows_at(half, blk))
            return 0

        lax.fori_loop(0, 2, feat_body, 0)
        run(before, s)
        quarter = pl.ds(pl.multiple_of(x * GRAM, GRAM), GRAM)

        @pl.when(s == 4)
        def _():
            wn[:, CPAD:] = fb[0, quarter, :].T

        def both(p):
            cols = pl.ds(0, WIDE[p])
            ps[s, :, cols] = scores(p, theirs).astype(BF)
            rc(ps.at[s, :, cols], pr.at[s, :, cols], pair_sem + s, partner).start()
            run(between, s, p)
            ows[k, :, cols] = scores(p, mine)

        pl.when(s < 4)(lambda: both(0))
        pl.when(s >= 4)(lambda: both(1))
        run(after, s)
        return 0

    lax.fori_loop(0, 8, panel_step, 0)

    def pair_done(k):
        cols = pl.ds(0, WIDE[k // 4])
        rc(ps.at[k, :, cols], pr.at[k, :, cols], pair_sem + k, partner).wait_send()

    for k in range(8):
        drain.append(lambda k=k: pair_done(k))

    f1_out = pltpu.make_async_copy(fb.at[1], f1_hbm, lsem.at[1])
    f1_out.start()
    reduce3(1)
    gg[0].step3()
    reduce5(1)
    gg[0].step4()
    gg[0].step5()
    g0_out = pltpu.make_async_copy(gb.at[0], g_hbm.at[0], lsem.at[4])
    g0_out.start()

    tail = {
        1: [lambda: find_target(1)],
        4: [lambda: find_margin(1)],
        7: [lambda: find_grad(1)],
    }

    def first_gradient(tile):
        return lax.dot_general(gb[0, :, tile], fb[0], (((0,), (0,)), ((), ())), preferred_element_type=F32)

    def update_step(t, _):
        tile = pl.ds(pl.multiple_of(t * 128, 128), 128)
        wf[tile, :] = wf[tile, :] - RATE * first_gradient(tile)
        pltpu.make_async_copy(wf.at[tile], wp_hbm.at[tile], lsem.at[2]).start()
        run(tail, t)
        return 0

    lax.fori_loop(0, TILES - 1, update_step, 0)
    tail_rows[...] = tail_rows[...] - RATE * first_gradient(pl.ds(LAST, 128))
    wp_last = pltpu.make_async_copy(tail_rows, wp_hbm.at[pl.ds(LAST, 128)], lsem.at[5])
    wp_last.start()
    gg[1].step1()
    gg[1].step2()
    gg[1].step3()
    gg[1].step4()
    gg[1].step5()
    g1_out = pltpu.make_async_copy(gb.at[1], g_hbm.at[1], lsem.at[3])
    g1_out.start()
    for fn in drain:
        fn()
    f1_out.wait()
    most = pl.ds(0, LAST)
    pltpu.make_async_copy(wf.at[most], wp_hbm.at[most], lsem.at[2]).wait()
    wp_last.wait()
    g0_out.wait()
    g1_out.wait()


def last_kernel(w, f, g, l0, l1, out, loss):
    gradient = lax.dot_general(g[0], f[...], (((0,), (0,)), ((), ())), preferred_element_type=F32)
    out[...] = w[...] - RATE * gradient

    @pl.when(pl.program_id(0) == 0)
    def _():
        lane = lax.broadcasted_iota(jnp.int32, (FRAMES, 128), 1)
        first = CLS - 1152
        here = (lane >= first) & (lane < first + 3)
        for p, ref in ((0, l0), (1, l1)):
            loss[p] = jnp.sum(jnp.where(here, ref[0].astype(F32), 0.0))


def per_device(inputs, projection, offsets, labels, weights):
    vm = pl.BlockSpec(memory_space=pltpu.VMEM)
    hbm = pl.BlockSpec(memory_space=pl.ANY)
    v = pltpu.VMEM
    wide = WIDE
    f1, g, wp = pl.pallas_call(
        step_kernel,
        out_shape=(
            jax.ShapeDtypeStruct((FRAMES, FEATS), BF),
            jax.ShapeDtypeStruct((2, FRAMES, CPAD), BF),
            jax.ShapeDtypeStruct((CPAD, FEATS), F32),
        ),
        in_specs=[vm, hbm, vm, vm, hbm],
        out_specs=(hbm, hbm, hbm),
        scratch_shapes=[
            v((2, FRAMES, DPAD), BF), v((DPAD, FEATS), BF), v((CLS, FEATS), F32), v((128, FEATS), F32), v((FEATS, WIDE[1]), BF),
            v((2, FRAMES, FEATS), BF), v((4, 128, WIDE[1]), F32),
            v((8, 128, WIDE[1]), BF), v((8, 128, WIDE[1]), BF),
            *[v((3, 128, w), BF) for w in wide], *[v((384, w), BF) for w in wide],
            *[v((96, w), BF) for w in wide], *[v((96, w), BF) for w in wide],
            *[v((128, w), F32) for w in wide],
            v((2, 32, CPAD), F32), v((4, 64, GRAM), BF),
            v((2, 4, 32, 128), F32), v((2, 4, 32, 128), F32), v((2, 128, 128), F32),
            v((2, FRAMES, CPAD), BF),
            pltpu.SemaphoreType.DMA((SEMS,)), pltpu.SemaphoreType.DMA((SEMS,)), pltpu.SemaphoreType.DMA((6,)),
        ],
        compiler_params=pltpu.CompilerParams(collective_id=0, has_side_effects=True, vmem_limit_bytes=65 * 1000 * 1000),
        name="panels",
    )(inputs, projection, offsets.reshape(1, FEATS), labels, weights.T)
    new, loss = pl.pallas_call(
        last_kernel,
        grid=(5,),
        out_shape=(jax.ShapeDtypeStruct((CLS, FEATS), F32), jax.ShapeDtypeStruct((2,), F32)),
        in_specs=[
            pl.BlockSpec((256, FEATS), lambda i: (i, 0)),
            pl.BlockSpec((FRAMES, FEATS), lambda i: (0, 0)),
            pl.BlockSpec((1, FRAMES, 256), lambda i: (1, 0, i)),
            pl.BlockSpec((1, FRAMES, 128), lambda i: (0, 0, 9)),
            pl.BlockSpec((1, FRAMES, 128), lambda i: (1, 0, 9)),
        ],
        out_specs=(pl.BlockSpec((256, FEATS), lambda i: (i, 0)), pl.BlockSpec(memory_space=pltpu.SMEM)),
        compiler_params=pltpu.CompilerParams(vmem_limit_bytes=62 * 2**20),
        name="last_update",
    )(wp, f1, g, g, g)
    return new.T, loss


def solution(mesh):
    return jax.shard_map(
        per_device,
        mesh=mesh,
        in_specs=(P(None, "feat", None), P(None, "feat"), P("feat"), P(), P("feat", "cls")),
        out_specs=(P("feat", "cls"), P()),
        check_vma=False,
    )
```

```python
import math

import jax
import jax.numpy as jnp
from jax import lax
from jax.experimental import pallas as pl
from jax.experimental.pallas import tpu as pltpu
from jax.sharding import PartitionSpec as P

DIN, DPAD = 360, 384
NFEAT = 65536
NCLS = 5000
FRAMES = 1024
FEATS = 2048
CLS = 1250
CPAD = 1280
GRAM = 256
TILES = 10
LAST = 1152
HALF = 640
SENDS, RECVS = 16, 96
WIDE = (CPAD, CPAD + GRAM)
RATE = 10.0
MESH = pl.DeviceIdType.MESH
BF, F32 = jnp.bfloat16, jnp.float32
SINE = (6.2831851595779975, -41.34165492085313, 81.60099762206104, -76.54964291002278, 39.53570242669577)


def m4(v):
    return lax.rem(v, 4)


def step_kernel(
    inp, proj, off, lab, w_hbm,
    f1_hbm, g1_hbm, l0_hbm, wp_hbm,
    xb, pb, wf, tail_rows, wn, fb, ows, ps, pr,
    s1_0, s1_1, r1_0, r1_1, s2_0, s2_1, r2_0, r2_1, own_0, own_1,
    so, kg, tg, ox, lt, lc, gb, ssem, rsem, lsem,
):
    feat, x = lax.axis_index("feat"), lax.axis_index("cls")
    c = lax.rem(feat, 2)
    y = m4(feat // 2)
    z = feat // 8
    p1 = y * (1 - c) + z * c
    p2 = z * (1 - c) + y * c

    def at(a, b):
        return ((b * (1 - c) + a * c) * 8 + (a * (1 - c) + b * c) * 2 + c, x)

    right1, left1 = at(m4(p1 + 1), p2), at(m4(p1 + 3), p2)
    across1 = at(m4(p1 + 2), p2)
    ring2 = [at(p1, m4(p2 + d)) for d in (1, 2, 3)]
    partner = (feat + 1 - 2 * c, x)
    others_x = [(feat, m4(x + j)) for j in (1, 2, 3)]

    drain = []

    def rc(src, dst, i, dev, j):
        return pltpu.make_async_remote_copy(
            src_ref=src,
            dst_ref=dst,
            send_sem=ssem.at[i],
            recv_sem=rsem.at[j],
            device_id=dev,
            device_id_type=MESH,
        )

    def sent(region, i):
        drain.append(lambda: rc(region(), region(), i, partner, 0).wait_send())

    def recv(region, i):
        rc(region, region, 0, partner, i).wait_recv()

    counter = [0]

    def sems(n):
        counter[0] += n
        return counter[0] - n

    group = [0]

    def send_sem():
        group[0] += 1
        return group[0] - 1

    def rows_at(cc, b1, b2=0, extra=0, size=128):
        start = cc * 512 + b1 * 128 + b2 * 32 + extra
        return pl.ds(pl.multiple_of(start, min(size, 128)), size)

    w_in = pltpu.make_async_copy(w_hbm, wf, lsem.at[4])
    proj_in = pltpu.make_async_copy(proj, pb.at[pl.ds(0, DIN)], lsem.at[0])
    proj_in.start()
    w_in.start()
    tail_rows[...] = jnp.zeros((128, FEATS), F32)

    own = lambda: rows_at(c, p1, p2, 0, 32)
    for p in range(2):
        xb[p, own(), :] = jnp.zeros((32, DPAD), BF)
        xb[p, own(), 0:DIN] = inp[p]

    barrier = pltpu.get_barrier_semaphore()
    for dev in [right1, left1, across1, partner] + ring2 + others_x:
        pl.semaphore_signal(barrier, inc=1, device_id=dev, device_id_type=MESH)
    pl.semaphore_wait(barrier, 10)

    class Gather:
        def __init__(self, buf, p, cols, direct):
            self.at = lambda rows: buf.at[p, rows, cols]
            self.direct = direct
            self.base, self.out = sems(13), send_sem()
            sent(lambda: self.at(pl.ds(0, 992)), self.out)

        def put(self, rows, i, dev):
            rc(self.at(rows()), self.at(rows()), self.out, dev, self.base + i).start()

        def take(self, rows, i):
            recv(self.at(rows()), self.base + i)

        def pass_on(self, rows):
            self.put(rows, 12, partner)

        def out1(self, j):
            rows = lambda: rows_at(c, p1, m4(p2 + j), 0, 32)
            self.put(rows, 3 + 2 * j, right1)
            self.put(rows, 4 + 2 * j, left1)
            if self.direct:
                self.put(rows, 11, across1)
            self.pass_on(rows)

        def in1(self, j):
            b2 = m4(p2 + j)
            self.take(lambda: rows_at(c, m4(p1 + 3), b2, 0, 32), 3 + 2 * j)
            if not self.direct:
                self.put(lambda: rows_at(c, m4(p1 + 3), b2, 0, 16), 11, right1)
            self.pass_on(lambda: rows_at(c, m4(p1 + 3), b2, 0, 32))
            self.take(lambda: rows_at(c, m4(p1 + 1), b2, 0, 32), 4 + 2 * j)
            if not self.direct:
                self.put(lambda: rows_at(c, m4(p1 + 1), b2, 16, 16), 11, left1)
            self.pass_on(lambda: rows_at(c, m4(p1 + 1), b2, 0, 32))

        def step0(self):
            for d in (2, 1, 3):
                self.put(own, d - 1, ring2[d - 1])
            self.out1(0)

        def step1(self):
            for d in (1, 3, 2):
                self.take(lambda: rows_at(c, p1, m4(p2 + 4 - d), 0, 32), d - 1)
                self.out1(4 - d)

        def step2(self):
            self.in1(0)

        def step3(self):
            for j in (3, 1, 2):
                self.in1(j)

        def step4(self):
            self.take(lambda: rows_at(c, m4(p1 + 2)), 11)
            self.pass_on(lambda: rows_at(c, m4(p1 + 2)))

        def step5(self):
            self.take(lambda: rows_at(1 - c, 0, 0, 0, 512), 12)

    gx = [Gather(xb, p, pl.ds(0, DPAD), True) for p in range(2)]
    gg = [Gather(gb, 0, pl.ds(0, CPAD), False)]
    ga = Gather(gb, 1, pl.ds(0, HALF), False)
    gz = Gather(gb, 1, pl.ds(HALF, CPAD - HALF), False)

    gx[0].step0()

    pb[DIN:DPAD, :] = jnp.zeros((DPAD - DIN, FEATS), BF)
    turns = off[...].astype(F32) * F32(1.0 / 65521.0)
    for q in range(FRAMES // 128):
        row = lab[0:1, q * 128:q * 128 + 128].astype(F32)
        turned = jnp.broadcast_to(row, (128, 128)).T
        for i in range(4):
            owner = 4 * q + i
            cc, yy, zz = owner % 2, owner // 2 % 4, owner // 8
            b1, b2 = (zz, yy) if cc else (yy, zz)
            start = cc * 512 + b1 * 128 + b2 * 32
            lc[start:start + 32, :] = turned[32 * i:32 * i + 32, :]
    lab_col = pl.multiple_of((feat // 4) * 128, 128)
    lt[...] = jnp.broadcast_to(lab[1:2, pl.ds(lab_col, 128)].astype(F32), (128, 128)).T

    def narrow(t):
        if t < TILES - 1:
            rows = wf[pl.ds(t * 128, 128), :]
        else:
            tail_rows[0:CLS - LAST, :] = wf[LAST:CLS, :]
            rows = tail_rows[...]
        wn[:, t * 128:t * 128 + 128] = rows.astype(BF).T

    w_in.wait()
    for t in range(5):
        narrow(t)
    gx[0].step1()
    gx[1].step0()
    for t in range(5, 8):
        narrow(t)
    gx[0].step2()
    gx[0].step3()
    gx[0].step4()
    for t in range(8, TILES):
        narrow(t)
    gx[1].step1()
    proj_in.wait()
    gx[0].step5()

    col = lax.broadcasted_iota(jnp.int32, (32, CPAD), 1)
    lane = lax.broadcasted_iota(jnp.int32, (32, 128), 1)
    scale = math.sqrt(2.0 / NFEAT)
    coef = [F32(v * scale) for v in SINE]

    def features(p, rows):
        acc = jnp.dot(xb[p, rows, :], pb[...], preferred_element_type=F32)
        u = acc * F32(1.0 / (2.0 * math.pi)) + turns
        q = jnp.abs(u - jnp.round(u)) - 0.25
        q2 = q * q
        r = coef[4]
        for v in coef[3::-1]:
            r = r * q2 + v
        fb[p, rows, :] = (r * q).astype(BF)

    def scores(p, rows):
        return jnp.dot(fb[p, rows, :], wn[:, 0:WIDE[p]], preferred_element_type=F32)

    S1, R1, S2, R2, OWN = (s1_0, s1_1), (r1_0, r1_1), (s2_0, s2_1), (r2_0, r2_1), (own_0, own_1)
    pair_sem = sems(8)
    ring_sem = [sems(7), sems(7)]
    tg_sem, ox_sem, kg_sem = [sems(1), sems(1)], [sems(1), sems(1)], sems(1)
    pair_out, ring_out, piece_out = ([send_sem(), send_sem()] for _ in range(3))
    tg_out, ox_out, kg_out = [send_sem(), send_sem()], [send_sem(), send_sem()], send_sem()
    three = pl.ds(0, 3)
    for p in range(2):
        sent(lambda p=p: ps.at[pl.ds(4 * p, 4), :, pl.ds(0, WIDE[p])], pair_out[p])
        sent(lambda p=p: R1[p], ring_out[p])
        sent(lambda p=p: R2[p], piece_out[p])
        sent(lambda p=p: tg.at[p, three], tg_out[p])
        sent(lambda p=p: ox.at[p, three], ox_out[p])
    sent(lambda: kg.at[three], kg_out)

    def pair_recv(p, k):
        recv(pr.at[4 * p + k, :, pl.ds(0, WIDE[p])], pair_sem + 4 * p + k)

    def apart(tile):
        at_lane = lax.broadcasted_iota(jnp.int32, tile.shape, 1)
        here = (at_lane == CLS - LAST) | (at_lane == CLS - LAST + 1)
        return jnp.sum(jnp.where(here, tile, 0.0), axis=1, keepdims=True)

    def rounded(p, v):
        if p:
            return v.astype(BF)
        tile = v[:, LAST:CPAD]
        at_lane = lax.broadcasted_iota(jnp.int32, tile.shape, 1)
        part = apart(tile)
        high = part.astype(BF).astype(F32)
        tile = jnp.where(at_lane == CLS - LAST, high, jnp.where(at_lane == CLS - LAST + 1, part - high, tile))
        return jnp.concatenate([v[:, 0:LAST], tile], axis=1).astype(BF)

    def mark_target(ref, i, rows):
        label = lc[rows, 0:1].astype(jnp.int32) - x * CLS
        label = jnp.where(label < CLS, label, -1)
        lane_at = lax.broadcasted_iota(jnp.int32, (128, 128), 1)
        found = jnp.zeros((128, 128), F32)
        for j in range(CPAD // 128):
            found += jnp.where(lane_at == label - j * 128, ref[i, :, j * 128:j * 128 + 128], 0.0)
        part = jnp.sum(found, axis=1, keepdims=True)
        ref[i, :, LAST:CPAD] = jnp.where(lane_at == CLS - LAST, part, ref[i, :, LAST:CPAD])

    def combine(p, k, put, lo, hi):
        def body(i, _):
            rows = pl.ds(pl.multiple_of(i * 32, 32), 32)
            put(rows, slice(0, WIDE[p]), ows[k, rows, 0:WIDE[p]] + pr[4 * p + k, rows, 0:WIDE[p]].astype(F32))
            return 0

        lax.fori_loop(lo, hi, body, 0)

    def reduce0(p):
        pair_recv(p, 0)
        s, r, i = S1[p], R1[p], ring_sem[p]

        def put(rows, cols, v):
            s[0, rows, cols] = rounded(p, v)

        combine(p, 0, put, 0, 4)
        rc(s.at[0, pl.ds(0, 64)], r.at[pl.ds(0, 64)], ring_out[p], right1, i).start()
        rc(s.at[0, pl.ds(64, 64)], r.at[pl.ds(64, 64)], ring_out[p], left1, i + 1).start()

    def reduce1(p):
        pair_recv(p, 1)
        s, r, i = S1[p], R1[p], ring_sem[p]
        recv(r.at[pl.ds(0, 64)], i)

        def put_in(rows, cols, v):
            s[1, rows, cols] = rounded(p, v + r[rows, cols].astype(F32))

        def put(rows, cols, v):
            s[1, rows, cols] = rounded(p, v)

        combine(p, 1, put_in, 0, 2)
        combine(p, 1, put, 2, 4)
        rc(s.at[1], r.at[pl.ds(128, 128)], ring_out[p], right1, i + 2).start()

    def reduce2(p):
        pair_recv(p, 2)
        s, r, i = S1[p], R1[p], ring_sem[p]
        recv(r.at[pl.ds(64, 64)], i + 1)

        def put_in(rows, cols, v):
            s[2, rows, cols] = rounded(p, v + r[rows, cols].astype(F32))

        def put(rows, cols, v):
            s[2, rows, cols] = rounded(p, v)

        combine(p, 2, put, 0, 2)
        combine(p, 2, put_in, 2, 4)
        rc(s.at[2], r.at[pl.ds(256, 128)], ring_out[p], left1, i + 3).start()

    def sub(d, extra=0, size=32):
        return pl.ds(pl.multiple_of(m4(p2 + d) * 32 + extra, 16), size)

    def reduce3(p):
        pair_recv(p, 3)
        r, i, o = R1[p], ring_sem[p], OWN[p]
        recv(r.at[pl.ds(128, 128)], i + 2)
        recv(r.at[pl.ds(256, 128)], i + 3)

        def put(rows, cols, v):
            a = pl.ds(pl.multiple_of(rows.start + 128, 32), 32)
            b = pl.ds(pl.multiple_of(rows.start + 256, 32), 32)
            o[rows, cols] = v + r[a, cols].astype(F32) + r[b, cols].astype(F32)

        combine(p, 3, put, 0, 4)
        s, r = S2[p], R2[p]
        for d in (2, 1, 3):
            piece = pl.ds(32 * d - 32, 32)
            s[piece, :] = rounded(p, o[sub(d), :])
            rc(s.at[piece], r.at[piece], piece_out[p], ring2[d - 1], i + 3 + d).start()

    def x_send(ref, out, i):
        for j in range(3):
            rc(ref.at[x], ref.at[x], out, others_x[j], i).start()

    def x_recv(ref, i):
        recv(ref.at[three], i)

    def reduce5(p):
        r, i, o = R2[p], ring_sem[p], OWN[p]
        total = o[sub(0), :]
        for d in (1, 3, 2):
            piece = pl.ds(32 * d - 32, 32)
            recv(r.at[piece], i + 3 + d)
            total += r[piece, :].astype(F32)
        so[p] = total[:, 0:CPAD]
        if p:
            k12 = total[:, CPAD:]
            high = k12.astype(BF)
            kg[x, 0:32, :] = high
            kg[x, 32:64, :] = (k12 - high.astype(F32)).astype(BF)
            x_send(kg, kg_out, kg_sem)

    lab_rows = pl.ds(pl.multiple_of(m4(feat) * 32, 32), 32)

    def is_target(p):
        label = (lt[lab_rows, 0:1] if p else lc[own(), 0:1]).astype(jnp.int32) - x * CLS
        return (col == label) & (col < CLS)

    def find_target(p):
        if p:
            x_recv(kg, kg_sem)
            moved = jnp.zeros((64, CPAD), F32)
            for j in range(4):
                moved += jnp.dot(kg[j], gb[0, j * GRAM:(j + 1) * GRAM, :], preferred_element_type=F32)
            so[p] = so[p] - RATE * (moved[0:32] + moved[32:64])
        if p:
            part = jnp.sum(jnp.where(is_target(p), so[p], 0.0), axis=1, keepdims=True)
        else:
            part = apart(so[0, :, LAST:])
        tg[p, x] = jnp.broadcast_to(part, (32, 128))
        x_send(tg.at[p], tg_out[p], tg_sem[p])

    def find_margin(p):
        x_recv(tg.at[p], tg_sem[p])
        target = (tg[p, 0] + tg[p, 1] + tg[p, 2] + tg[p, 3])[:, 0:1]
        keep = (col < CLS) & jnp.logical_not(is_target(p))
        margin = jnp.where(keep, jnp.maximum(0.0, 1.0 + so[p] - target), 0.0)
        slope = margin * F32(2.0 / (NCLS - 1))
        so[p] = slope
        out = jnp.sum(slope, axis=1, keepdims=True)
        loss = jnp.sum(margin * margin, axis=1, keepdims=True) * F32(1.0 / (NCLS - 1))
        ox[p, x] = jnp.where(lane < 64, out, loss)
        x_send(ox.at[p], ox_out[p], ox_sem[p])

    def find_grad(p):
        x_recv(ox.at[p], ox_sem[p])
        both = ox[p, 0] + ox[p, 1] + ox[p, 2] + ox[p, 3]
        out, loss = both[:, 0:1], both[:, 64:65]
        high = loss.astype(BF).astype(F32)
        mid = (loss - high).astype(BF).astype(F32)
        low = loss - high - mid
        g = jnp.where(is_target(p), -out, so[p])
        g = jnp.where(col == CLS, high, g)
        g = jnp.where(col == CLS + 1, mid, g)
        g = jnp.where(col == CLS + 2, low, g)
        gb[p, own(), :] = g.astype(BF)
        if p:
            ga.step0()
            gz.step0()
        else:
            gg[0].step0()

    before = {
        1: [lambda: reduce0(0)],
        2: [lambda: reduce1(0)],
        3: [lambda: reduce2(0)],
        4: [lambda: reduce3(0)],
        5: [lambda: reduce5(0), lambda: find_target(0), lambda: reduce0(1)],
        6: [lambda: find_grad(0), lambda: reduce1(1)],
        7: [lambda: reduce2(1), lambda: gg[0].step1()],
    }
    between = {
        0: [lambda: gx[1].step2()],
        1: [lambda: gx[1].step3()],
        2: [lambda: gx[1].step4()],
        3: [lambda: gx[1].step5()],
        7: [lambda: gg[0].step2()],
    }
    after = {
        5: [lambda: find_margin(0)],
    }

    def run(tasks, s, panel=None):
        for at_step, fns in tasks.items():
            if panel is not None and at_step // 4 != panel:
                continue

            @pl.when(s == at_step)
            def _(fns=fns):
                for fn in fns:
                    fn()

    def panel_step(s, _):
        p, k = s // 4, lax.rem(s, 4)
        d = 2 - k + 3 * (k // 2) - 2 * (k // 3)
        theirs = rows_at(1 - c, m4(p2 + d))
        mine = rows_at(c, m4(p1 + d))

        features(p, theirs)
        features(p, mine)
        run(before, s)
        quarter = pl.ds(pl.multiple_of(x * GRAM, GRAM), GRAM)

        @pl.when(s == 4)
        def _():
            wn[:, CPAD:] = fb[0, quarter, :].T

        def both(p):
            cols = pl.ds(0, WIDE[p])
            ps[s, :, cols] = scores(p, theirs)
            if p == 0:
                mark_target(ps, s, theirs)
            rc(ps.at[s, :, cols], pr.at[s, :, cols], pair_out[p], partner, pair_sem + s).start()
            run(between, s, p)
            ows[k, :, cols] = scores(p, mine)
            if p == 0:
                mark_target(ows, k, mine)

        pl.when(s < 4)(lambda: both(0))
        pl.when(s >= 4)(lambda: both(1))
        run(after, s)
        return 0

    lax.fori_loop(0, 8, panel_step, 0)

    f1_out = pltpu.make_async_copy(fb.at[1], f1_hbm, lsem.at[1])
    f1_out.start()
    reduce3(1)
    gg[0].step3()
    reduce5(1)
    gg[0].step4()
    gg[0].step5()
    g0_out = pltpu.make_async_copy(gb.at[0, :, pl.ds(LAST, 128)], l0_hbm, lsem.at[4])
    g0_out.start()

    tail = {
        1: [lambda: find_target(1)],
        4: [lambda: find_margin(1)],
        7: [lambda: find_grad(1)],
    }

    def gradient(p, tile):
        return lax.dot_general(gb[p, :, tile], fb[p], (((0,), (0,)), ((), ())), preferred_element_type=F32)

    def update_step(t, _):
        tile = pl.ds(pl.multiple_of(t * 128, 128), 128)
        wf[tile, :] = wf[tile, :] - RATE * gradient(0, tile)

        @pl.when(t >= HALF // 128)
        def _():
            pltpu.make_async_copy(wf.at[tile], wp_hbm.at[tile], lsem.at[2]).start()

        run(tail, t)
        return 0

    lax.fori_loop(0, TILES - 1, update_step, 0)
    tail_rows[...] = tail_rows[...] - RATE * gradient(0, pl.ds(LAST, 128))
    wp_last = pltpu.make_async_copy(tail_rows, wp_hbm.at[pl.ds(LAST, 128)], lsem.at[5])
    wp_last.start()
    ga.step1()
    gz.step1()
    ga.step2()
    ga.step3()
    gz.step2()
    gz.step3()
    ga.step4()
    ga.step5()
    second = {0: [lambda: gz.step4()]}

    def second_step(t, _):
        tile = pl.ds(pl.multiple_of(t * 128, 128), 128)
        run(second, t)
        wf[tile, :] = wf[tile, :] - RATE * gradient(1, tile)
        pltpu.make_async_copy(wf.at[tile], wp_hbm.at[tile], lsem.at[2]).start()
        return 0

    lax.fori_loop(0, HALF // 128, second_step, 0)
    gz.step5()
    g1_out = pltpu.make_async_copy(gb.at[1, :, pl.ds(HALF, CPAD - HALF)], g1_hbm, lsem.at[3])
    g1_out.start()
    for fn in drain:
        fn()
    f1_out.wait()
    most = pl.ds(0, LAST)
    pltpu.make_async_copy(wf.at[most], wp_hbm.at[most], lsem.at[2]).wait()
    wp_last.wait()
    g0_out.wait()
    g1_out.wait()


def block_of(i):
    return i // 2 + 5 * (1 - lax.rem(i, 2))


def last_kernel(w_hbm, f_hbm, g_hbm, l0, out, loss, wf, f, g, sem):
    i = pl.program_id(0)
    f_in = pltpu.make_async_copy(f_hbm, f, sem.at[0])
    g_in = pltpu.make_async_copy(g_hbm, g, sem.at[1])

    def load(t):
        rows = pl.ds(pl.multiple_of(t * 128, 128), 128)
        return pltpu.make_async_copy(w_hbm.at[rows], wf.at[rows], sem.at[2 + t])

    @pl.when(i == 0)
    def _():
        g_in.start()
        f_in.start()
        for t in (5, 0, 6, 1, 7, 2, 8, 3, 9, 4):
            load(t).start()
        g_in.wait()
        lane = lax.broadcasted_iota(jnp.int32, (FRAMES, 128), 1)
        first = CLS - LAST
        here = (lane >= first) & (lane < first + 3)
        loss[0] = jnp.sum(jnp.where(here, l0[...].astype(F32), 0.0))
        loss[1] = jnp.sum(jnp.where(here, g[:, LAST - HALF:].astype(F32), 0.0))
        f_in.wait()

    block = block_of(i)
    load(block).wait()
    rows = pl.ds(pl.multiple_of(block * 128, 128), 128)

    @pl.when(lax.rem(i, 2) == 0)
    def _():
        cols = pl.ds(pl.multiple_of(block * 128 - HALF, 128), 128)
        gradient = lax.dot_general(g[:, cols], f[...], (((0,), (0,)), ((), ())), preferred_element_type=F32)
        out[...] = wf[rows, :] - RATE * gradient

    @pl.when(lax.rem(i, 2) == 1)
    def _():
        out[...] = wf[rows, :]


def per_device(inputs, projection, offsets, labels, weights):
    vm = pl.BlockSpec(memory_space=pltpu.VMEM)
    hbm = pl.BlockSpec(memory_space=pl.ANY)
    v = pltpu.VMEM
    wide = WIDE
    f1, g1, l0, wp = pl.pallas_call(
        step_kernel,
        out_shape=(
            jax.ShapeDtypeStruct((FRAMES, FEATS), BF),
            jax.ShapeDtypeStruct((FRAMES, CPAD - HALF), BF),
            jax.ShapeDtypeStruct((FRAMES, 128), BF),
            jax.ShapeDtypeStruct((CPAD, FEATS), F32),
        ),
        in_specs=[vm, hbm, vm, vm, hbm],
        out_specs=(hbm, hbm, hbm, hbm),
        scratch_shapes=[
            v((2, FRAMES, DPAD), BF), v((DPAD, FEATS), BF), v((CLS, FEATS), F32), v((128, FEATS), F32), v((FEATS, WIDE[1]), BF),
            v((2, FRAMES, FEATS), BF), v((4, 128, WIDE[1]), F32),
            v((8, 128, WIDE[1]), F32), v((8, 128, WIDE[1]), F32),
            *[v((3, 128, w), BF) for w in wide], *[v((384, w), BF) for w in wide],
            *[v((96, w), BF) for w in wide], *[v((96, w), BF) for w in wide],
            *[v((128, w), F32) for w in wide],
            v((2, 32, CPAD), F32), v((4, 64, GRAM), BF),
            v((2, 4, 32, 128), F32), v((2, 4, 32, 128), F32), v((128, 128), F32), v((FRAMES, 128), F32),
            v((2, FRAMES, CPAD), BF),
            pltpu.SemaphoreType.DMA((SENDS,)), pltpu.SemaphoreType.DMA((RECVS,)), pltpu.SemaphoreType.DMA((6,)),
        ],
        compiler_params=pltpu.CompilerParams(collective_id=0, has_side_effects=True, vmem_limit_bytes=65 * 1000 * 1000),
        name="panels",
    )(inputs, projection, offsets.reshape(1, FEATS), labels, weights.T)
    new, loss = pl.pallas_call(
        last_kernel,
        grid=(TILES,),
        out_shape=(jax.ShapeDtypeStruct((CLS, FEATS), F32), jax.ShapeDtypeStruct((2,), F32)),
        in_specs=[hbm, hbm, hbm, pl.BlockSpec((FRAMES, 128), lambda i: (0, 0))],
        out_specs=(
            pl.BlockSpec((128, FEATS), lambda i: (block_of(i), 0)),
            pl.BlockSpec(memory_space=pltpu.SMEM),
        ),
        scratch_shapes=[
            v((CPAD, FEATS), F32), v((FRAMES, FEATS), BF), v((FRAMES, CPAD - HALF), BF),
            pltpu.SemaphoreType.DMA((2 + TILES,)),
        ],
        compiler_params=pltpu.CompilerParams(vmem_limit_bytes=62 * 2**20),
        name="last_update",
    )(wp, f1, g1, l0)
    return new.T, loss


def solution(mesh):
    return jax.shard_map(
        per_device,
        mesh=mesh,
        in_specs=(P(None, "feat", None), P(None, "feat"), P("feat"), P(), P("feat", "cls")),
        out_specs=(P("feat", "cls"), P()),
        check_vma=False,
    )
```

```python
import math

import jax
import jax.numpy as jnp
from jax import lax
from jax.experimental import pallas as pl
from jax.experimental.pallas import tpu as pltpu
from jax.sharding import PartitionSpec as P

DIN, DPAD = 360, 384
NFEAT = 65536
NCLS = 5000
FRAMES = 1024
FEATS = 2048
CLS = 1250
CPAD = 1280
GRAM = 256
TILES = 10
LAST = 1152
HALF = 640
SENDS, RECVS = 16, 96
WIDE = (CPAD, CPAD + GRAM)
RATE = 10.0
MESH = pl.DeviceIdType.MESH
BF, F32 = jnp.bfloat16, jnp.float32
SINE = (6.2831851595779975, -41.34165492085313, 81.60099762206104, -76.54964291002278, 39.53570242669577)


def m4(v):
    return lax.rem(v, 4)


def step_kernel(
    inp, proj, off, lab, w_hbm,
    fb, gb, wf, tail_rows,
    xb, pb, wn, ows, ps, pr,
    s1_0, s1_1, r1_0, r1_1, s2_0, s2_1, r2_0, r2_1, own_0, own_1,
    so, kg, tg, ox, lt, lc, ssem, rsem, lsem,
):
    feat, x = lax.axis_index("feat"), lax.axis_index("cls")
    c = lax.rem(feat, 2)
    y = m4(feat // 2)
    z = feat // 8
    p1 = y * (1 - c) + z * c
    p2 = z * (1 - c) + y * c

    def at(a, b):
        return ((b * (1 - c) + a * c) * 8 + (a * (1 - c) + b * c) * 2 + c, x)

    right1, left1 = at(m4(p1 + 1), p2), at(m4(p1 + 3), p2)
    across1 = at(m4(p1 + 2), p2)
    ring2 = [at(p1, m4(p2 + d)) for d in (1, 2, 3)]
    partner = (feat + 1 - 2 * c, x)
    others_x = [(feat, m4(x + j)) for j in (1, 2, 3)]

    drain = []

    def rc(src, dst, i, dev, j):
        return pltpu.make_async_remote_copy(
            src_ref=src,
            dst_ref=dst,
            send_sem=ssem.at[i],
            recv_sem=rsem.at[j],
            device_id=dev,
            device_id_type=MESH,
        )

    def sent(region, i):
        drain.append(lambda: rc(region(), region(), i, partner, 0).wait_send())

    def recv(region, i):
        rc(region, region, 0, partner, i).wait_recv()

    counter = [0]

    def sems(n):
        counter[0] += n
        return counter[0] - n

    group = [0]

    def send_sem():
        group[0] += 1
        return group[0] - 1

    def rows_at(cc, b1, b2=0, extra=0, size=128):
        start = cc * 512 + b1 * 128 + b2 * 32 + extra
        return pl.ds(pl.multiple_of(start, min(size, 128)), size)

    barrier = pltpu.get_barrier_semaphore()
    for dev in [right1, left1, across1, partner] + ring2 + others_x:
        pl.semaphore_signal(barrier, inc=1, device_id=dev, device_id_type=MESH)

    w_in = pltpu.make_async_copy(w_hbm, wf, lsem.at[4])
    proj_in = pltpu.make_async_copy(proj, pb.at[pl.ds(0, DIN)], lsem.at[0])
    proj_in.start()
    w_in.start()
    tail_rows[...] = jnp.zeros((128, FEATS), F32)

    own = lambda: rows_at(c, p1, p2, 0, 32)
    for p in range(2):
        xb[p, own(), :] = jnp.zeros((32, DPAD), BF)
        xb[p, own(), 0:DIN] = inp[p]

    pl.semaphore_wait(barrier, 10)

    class Gather:
        def __init__(self, buf, p, cols, direct):
            self.at = lambda rows: buf.at[p, rows, cols]
            self.direct = direct
            self.base, self.out = sems(13), send_sem()
            sent(lambda: self.at(pl.ds(0, 992)), self.out)

        def put(self, rows, i, dev):
            rc(self.at(rows()), self.at(rows()), self.out, dev, self.base + i).start()

        def take(self, rows, i):
            recv(self.at(rows()), self.base + i)

        def pass_on(self, rows):
            self.put(rows, 12, partner)

        def out1(self, j):
            rows = lambda: rows_at(c, p1, m4(p2 + j), 0, 32)
            self.put(rows, 3 + 2 * j, right1)
            self.put(rows, 4 + 2 * j, left1)
            if self.direct:
                self.put(rows, 11, across1)
            self.pass_on(rows)

        def in1(self, j):
            b2 = m4(p2 + j)
            self.take(lambda: rows_at(c, m4(p1 + 3), b2, 0, 32), 3 + 2 * j)
            if not self.direct:
                self.put(lambda: rows_at(c, m4(p1 + 3), b2, 0, 16), 11, right1)
            self.pass_on(lambda: rows_at(c, m4(p1 + 3), b2, 0, 32))
            self.take(lambda: rows_at(c, m4(p1 + 1), b2, 0, 32), 4 + 2 * j)
            if not self.direct:
                self.put(lambda: rows_at(c, m4(p1 + 1), b2, 16, 16), 11, left1)
            self.pass_on(lambda: rows_at(c, m4(p1 + 1), b2, 0, 32))

        def step0(self):
            for d in (2, 1, 3):
                self.put(own, d - 1, ring2[d - 1])
            self.out1(0)

        def step1(self):
            for d in (1, 3, 2):
                self.take(lambda: rows_at(c, p1, m4(p2 + 4 - d), 0, 32), d - 1)
                self.out1(4 - d)

        def step2(self):
            self.in1(0)

        def step3(self):
            for j in (3, 1, 2):
                self.in1(j)

        def step4(self):
            self.take(lambda: rows_at(c, m4(p1 + 2)), 11)
            self.pass_on(lambda: rows_at(c, m4(p1 + 2)))

        def step5(self):
            self.take(lambda: rows_at(1 - c, 0, 0, 0, 512), 12)

    gx = [Gather(xb, p, pl.ds(0, DPAD), True) for p in range(2)]
    gg = [Gather(gb, 0, pl.ds(0, CPAD), False)]
    ga = Gather(gb, 1, pl.ds(0, HALF), False)
    gz = Gather(gb, 1, pl.ds(HALF, CPAD - HALF), False)

    gx[0].step0()

    pb[DIN:DPAD, :] = jnp.zeros((DPAD - DIN, FEATS), BF)
    turns = off[...].astype(F32) * F32(1.0 / 65521.0)
    for q in range(FRAMES // 128):
        row = lab[0:1, q * 128:q * 128 + 128].astype(F32)
        turned = jnp.broadcast_to(row, (128, 128)).T
        for i in range(4):
            owner = 4 * q + i
            cc, yy, zz = owner % 2, owner // 2 % 4, owner // 8
            b1, b2 = (zz, yy) if cc else (yy, zz)
            start = cc * 512 + b1 * 128 + b2 * 32
            lc[start:start + 32, :] = turned[32 * i:32 * i + 32, :]
    lab_col = pl.multiple_of((feat // 4) * 128, 128)
    lt[...] = jnp.broadcast_to(lab[1:2, pl.ds(lab_col, 128)].astype(F32), (128, 128)).T

    def narrow(t):
        if t < TILES - 1:
            rows = wf[pl.ds(t * 128, 128), :]
        else:
            tail_rows[0:CLS - LAST, :] = wf[LAST:CLS, :]
            rows = tail_rows[...]
        wn[:, t * 128:t * 128 + 128] = rows.astype(BF).T

    w_in.wait()
    for t in range(5):
        narrow(t)
    gx[0].step1()
    gx[1].step0()
    for t in range(5, 8):
        narrow(t)
    gx[0].step2()
    gx[0].step3()
    gx[0].step4()
    for t in range(8, TILES):
        narrow(t)
    gx[1].step1()
    proj_in.wait()
    gx[0].step5()

    col = lax.broadcasted_iota(jnp.int32, (32, CPAD), 1)
    lane = lax.broadcasted_iota(jnp.int32, (32, 128), 1)
    scale = math.sqrt(2.0 / NFEAT)
    coef = [F32(v * scale) for v in SINE]

    def features(p, rows):
        acc = jnp.dot(xb[p, rows, :], pb[...], preferred_element_type=F32)
        u = acc * F32(1.0 / (2.0 * math.pi)) + turns
        q = jnp.abs(u - jnp.round(u)) - 0.25
        q2 = q * q
        r = coef[4]
        for v in coef[3::-1]:
            r = r * q2 + v
        fb[p, rows, :] = (r * q).astype(BF)

    def scores(p, rows):
        return jnp.dot(fb[p, rows, :], wn[:, 0:WIDE[p]], preferred_element_type=F32)

    S1, R1, S2, R2, OWN = (s1_0, s1_1), (r1_0, r1_1), (s2_0, s2_1), (r2_0, r2_1), (own_0, own_1)
    pair_sem = sems(8)
    ring_sem = [sems(7), sems(7)]
    tg_sem, ox_sem, kg_sem = [sems(1), sems(1)], [sems(1), sems(1)], sems(1)
    pair_out, ring_out, piece_out = ([send_sem(), send_sem()] for _ in range(3))
    tg_out, ox_out, kg_out = [send_sem(), send_sem()], [send_sem(), send_sem()], send_sem()
    three = pl.ds(0, 3)
    for p in range(2):
        sent(lambda p=p: ps.at[pl.ds(4 * p, 4), :, pl.ds(0, WIDE[p])], pair_out[p])
        sent(lambda p=p: R1[p], ring_out[p])
        sent(lambda p=p: R2[p], piece_out[p])
        sent(lambda p=p: tg.at[p, three], tg_out[p])
        sent(lambda p=p: ox.at[p, three], ox_out[p])
    sent(lambda: kg.at[three], kg_out)

    def pair_recv(p, k):
        recv(pr.at[4 * p + k, :, pl.ds(0, WIDE[p])], pair_sem + 4 * p + k)

    def apart(tile):
        at_lane = lax.broadcasted_iota(jnp.int32, tile.shape, 1)
        here = (at_lane == CLS - LAST) | (at_lane == CLS - LAST + 1)
        return jnp.sum(jnp.where(here, tile, 0.0), axis=1, keepdims=True)

    def rounded(p, v):
        if p:
            return v.astype(BF)
        tile = v[:, LAST:CPAD]
        at_lane = lax.broadcasted_iota(jnp.int32, tile.shape, 1)
        part = apart(tile)
        high = part.astype(BF).astype(F32)
        tile = jnp.where(at_lane == CLS - LAST, high, jnp.where(at_lane == CLS - LAST + 1, part - high, tile))
        return jnp.concatenate([v[:, 0:LAST], tile], axis=1).astype(BF)

    def mark_target(ref, i, rows):
        label = lc[rows, 0:1].astype(jnp.int32) - x * CLS
        label = jnp.where(label < CLS, label, -1)
        lane_at = lax.broadcasted_iota(jnp.int32, (128, 128), 1)
        found = jnp.zeros((128, 128), F32)
        for j in range(CPAD // 128):
            found += jnp.where(lane_at == label - j * 128, ref[i, :, j * 128:j * 128 + 128], 0.0)
        part = jnp.sum(found, axis=1, keepdims=True)
        ref[i, :, LAST:CPAD] = jnp.where(lane_at == CLS - LAST, part, ref[i, :, LAST:CPAD])

    def combine(p, k, put, lo, hi):
        def body(i, _):
            rows = pl.ds(pl.multiple_of(i * 32, 32), 32)
            put(rows, slice(0, WIDE[p]), ows[k, rows, 0:WIDE[p]] + pr[4 * p + k, rows, 0:WIDE[p]].astype(F32))
            return 0

        lax.fori_loop(lo, hi, body, 0)

    def reduce0(p):
        pair_recv(p, 0)
        s, r, i = S1[p], R1[p], ring_sem[p]

        def put(rows, cols, v):
            s[0, rows, cols] = rounded(p, v)

        combine(p, 0, put, 0, 4)
        rc(s.at[0, pl.ds(0, 64)], r.at[pl.ds(0, 64)], ring_out[p], right1, i).start()
        rc(s.at[0, pl.ds(64, 64)], r.at[pl.ds(64, 64)], ring_out[p], left1, i + 1).start()

    def reduce1(p):
        pair_recv(p, 1)
        s, r, i = S1[p], R1[p], ring_sem[p]
        recv(r.at[pl.ds(0, 64)], i)

        def put_in(rows, cols, v):
            s[1, rows, cols] = rounded(p, v + r[rows, cols].astype(F32))

        def put(rows, cols, v):
            s[1, rows, cols] = rounded(p, v)

        combine(p, 1, put_in, 0, 2)
        combine(p, 1, put, 2, 4)
        rc(s.at[1], r.at[pl.ds(128, 128)], ring_out[p], right1, i + 2).start()

    def reduce2(p):
        pair_recv(p, 2)
        s, r, i = S1[p], R1[p], ring_sem[p]
        recv(r.at[pl.ds(64, 64)], i + 1)

        def put_in(rows, cols, v):
            s[2, rows, cols] = rounded(p, v + r[rows, cols].astype(F32))

        def put(rows, cols, v):
            s[2, rows, cols] = rounded(p, v)

        combine(p, 2, put, 0, 2)
        combine(p, 2, put_in, 2, 4)
        rc(s.at[2], r.at[pl.ds(256, 128)], ring_out[p], left1, i + 3).start()

    def sub(d, extra=0, size=32):
        return pl.ds(pl.multiple_of(m4(p2 + d) * 32 + extra, 16), size)

    def reduce3(p):
        pair_recv(p, 3)
        r, i, o = R1[p], ring_sem[p], OWN[p]
        recv(r.at[pl.ds(128, 128)], i + 2)
        recv(r.at[pl.ds(256, 128)], i + 3)

        def put(rows, cols, v):
            a = pl.ds(pl.multiple_of(rows.start + 128, 32), 32)
            b = pl.ds(pl.multiple_of(rows.start + 256, 32), 32)
            o[rows, cols] = v + r[a, cols].astype(F32) + r[b, cols].astype(F32)

        combine(p, 3, put, 0, 4)
        s, r = S2[p], R2[p]
        for d in (2, 1, 3):
            piece = pl.ds(32 * d - 32, 32)
            s[piece, :] = rounded(p, o[sub(d), :])
            rc(s.at[piece], r.at[piece], piece_out[p], ring2[d - 1], i + 3 + d).start()

    def x_send(ref, out, i):
        for j in range(3):
            rc(ref.at[x], ref.at[x], out, others_x[j], i).start()

    def x_recv(ref, i):
        recv(ref.at[three], i)

    def reduce5(p):
        r, i, o = R2[p], ring_sem[p], OWN[p]
        total = o[sub(0), :]
        for d in (1, 3, 2):
            piece = pl.ds(32 * d - 32, 32)
            recv(r.at[piece], i + 3 + d)
            total += r[piece, :].astype(F32)
        so[p] = total[:, 0:CPAD]
        if p:
            k12 = total[:, CPAD:]
            high = k12.astype(BF)
            kg[x, 0:32, :] = high
            kg[x, 32:64, :] = (k12 - high.astype(F32)).astype(BF)
            x_send(kg, kg_out, kg_sem)

    lab_rows = pl.ds(pl.multiple_of(m4(feat) * 32, 32), 32)

    def is_target(p):
        label = (lt[lab_rows, 0:1] if p else lc[own(), 0:1]).astype(jnp.int32) - x * CLS
        return (col == label) & (col < CLS)

    def find_target(p):
        if p:
            x_recv(kg, kg_sem)
            moved = jnp.zeros((64, CPAD), F32)
            for j in range(4):
                moved += jnp.dot(kg[j], gb[0, j * GRAM:(j + 1) * GRAM, :], preferred_element_type=F32)
            so[p] = so[p] - RATE * (moved[0:32] + moved[32:64])
        if p:
            part = jnp.sum(jnp.where(is_target(p), so[p], 0.0), axis=1, keepdims=True)
        else:
            part = apart(so[0, :, LAST:])
        tg[p, x] = jnp.broadcast_to(part, (32, 128))
        x_send(tg.at[p], tg_out[p], tg_sem[p])

    def find_margin(p):
        x_recv(tg.at[p], tg_sem[p])
        target = (tg[p, 0] + tg[p, 1] + tg[p, 2] + tg[p, 3])[:, 0:1]
        keep = (col < CLS) & jnp.logical_not(is_target(p))
        margin = jnp.where(keep, jnp.maximum(0.0, 1.0 + so[p] - target), 0.0)
        slope = margin * F32(2.0 / (NCLS - 1))
        so[p] = slope
        out = jnp.sum(slope, axis=1, keepdims=True)
        loss = jnp.sum(margin * margin, axis=1, keepdims=True) * F32(1.0 / (NCLS - 1))
        ox[p, x] = jnp.where(lane < 64, out, loss)
        x_send(ox.at[p], ox_out[p], ox_sem[p])

    def find_grad(p):
        x_recv(ox.at[p], ox_sem[p])
        both = ox[p, 0] + ox[p, 1] + ox[p, 2] + ox[p, 3]
        out, loss = both[:, 0:1], both[:, 64:65]
        high = loss.astype(BF).astype(F32)
        mid = (loss - high).astype(BF).astype(F32)
        low = loss - high - mid
        g = jnp.where(is_target(p), -out, so[p])
        g = jnp.where(col == CLS, high, g)
        g = jnp.where(col == CLS + 1, mid, g)
        g = jnp.where(col == CLS + 2, low, g)
        gb[p, own(), :] = g.astype(BF)
        if p:
            ga.step0()
            gz.step0()
        else:
            gg[0].step0()

    before = {
        1: [lambda: reduce0(0)],
        2: [lambda: reduce1(0)],
        3: [lambda: reduce2(0)],
        4: [lambda: reduce3(0)],
        5: [lambda: reduce5(0), lambda: find_target(0), lambda: reduce0(1)],
        6: [lambda: find_grad(0), lambda: reduce1(1)],
        7: [lambda: reduce2(1), lambda: gg[0].step1()],
    }
    between = {
        0: [lambda: gx[1].step2()],
        1: [lambda: gx[1].step3()],
        2: [lambda: gx[1].step4()],
        3: [lambda: gx[1].step5()],
        7: [lambda: gg[0].step2()],
    }
    after = {
        5: [lambda: find_margin(0)],
    }

    def run(tasks, s, panel=None):
        for at_step, fns in tasks.items():
            if panel is not None and at_step // 4 != panel:
                continue

            @pl.when(s == at_step)
            def _(fns=fns):
                for fn in fns:
                    fn()

    def panel_step(s, _):
        p, k = s // 4, lax.rem(s, 4)
        d = 2 - k + 3 * (k // 2) - 2 * (k // 3)
        theirs = rows_at(1 - c, m4(p2 + d))
        mine = rows_at(c, m4(p1 + d))

        features(p, theirs)
        features(p, mine)
        run(before, s)
        quarter = pl.ds(pl.multiple_of(x * GRAM, GRAM), GRAM)

        @pl.when(s == 4)
        def _():
            wn[:, CPAD:] = fb[0, quarter, :].T

        def both(p):
            cols = pl.ds(0, WIDE[p])
            ps[s, :, cols] = scores(p, theirs)
            if p == 0:
                mark_target(ps, s, theirs)
            rc(ps.at[s, :, cols], pr.at[s, :, cols], pair_out[p], partner, pair_sem + s).start()
            run(between, s, p)
            ows[k, :, cols] = scores(p, mine)
            if p == 0:
                mark_target(ows, k, mine)

        pl.when(s < 4)(lambda: both(0))
        pl.when(s >= 4)(lambda: both(1))
        run(after, s)
        return 0

    lax.fori_loop(0, 8, panel_step, 0)

    reduce3(1)
    gg[0].step3()
    reduce5(1)
    gg[0].step4()
    gg[0].step5()

    tail = {
        1: [lambda: find_target(1)],
        4: [lambda: find_margin(1)],
        7: [lambda: find_grad(1)],
    }

    def gradient(p, tile):
        return lax.dot_general(gb[p, :, tile], fb[p], (((0,), (0,)), ((), ())), preferred_element_type=F32)

    def update_step(t, _):
        tile = pl.ds(pl.multiple_of(t * 128, 128), 128)
        wf[tile, :] = wf[tile, :] - RATE * gradient(0, tile)

        run(tail, t)
        return 0

    lax.fori_loop(0, TILES - 1, update_step, 0)
    tail_rows[...] = tail_rows[...] - RATE * gradient(0, pl.ds(LAST, 128))
    ga.step1()
    gz.step1()
    ga.step2()
    ga.step3()
    gz.step2()
    gz.step3()
    ga.step4()
    ga.step5()
    second = {2: [lambda: gz.step4()]}

    def second_step(t, _):
        tile = pl.ds(pl.multiple_of(t * 128, 128), 128)
        run(second, t)
        wf[tile, :] = wf[tile, :] - RATE * gradient(1, tile)
        return 0

    lax.fori_loop(0, HALF // 128, second_step, 0)
    gz.step5()
    for fn in drain:
        fn()


def last_kernel(fb, gb, wf, tail_rows, out, loss):
    i = pl.program_id(0)

    @pl.when(i == 0)
    def _():
        lane = lax.broadcasted_iota(jnp.int32, (FRAMES, 128), 1)
        first = CLS - LAST
        here = (lane >= first) & (lane < first + 3)
        for p in range(2):
            loss[p] = jnp.sum(jnp.where(here, gb[p, :, LAST:].astype(F32), 0.0))

    cols = pl.ds(pl.multiple_of(i * 128, 128), 128)

    @pl.when(i < HALF // 128)
    def _():
        out[...] = wf[cols, :]

    @pl.when(i >= HALF // 128)
    def _():
        gradient = lax.dot_general(gb[1, :, cols], fb[1], (((0,), (0,)), ((), ())), preferred_element_type=F32)

        @pl.when(i < TILES - 1)
        def _():
            out[...] = wf[cols, :] - RATE * gradient

        @pl.when(i == TILES - 1)
        def _():
            out[...] = tail_rows[...] - RATE * gradient


def per_device(inputs, projection, offsets, labels, weights):
    vm = pl.BlockSpec(memory_space=pltpu.VMEM)
    hbm = pl.BlockSpec(memory_space=pl.ANY)
    v = pltpu.VMEM
    wide = WIDE
    kept = pl.pallas_call(
        step_kernel,
        out_shape=(
            v((2, FRAMES, FEATS), BF), v((2, FRAMES, CPAD), BF), v((CLS, FEATS), F32), v((128, FEATS), F32),
        ),
        in_specs=[vm, hbm, vm, vm, hbm],
        out_specs=(vm, vm, vm, vm),
        scratch_shapes=[
            v((2, FRAMES, DPAD), BF), v((DPAD, FEATS), BF), v((FEATS, WIDE[1]), BF),
            v((4, 128, WIDE[1]), F32),
            v((8, 128, WIDE[1]), F32), v((8, 128, WIDE[1]), F32),
            *[v((3, 128, w), BF) for w in wide], *[v((384, w), BF) for w in wide],
            *[v((96, w), BF) for w in wide], *[v((96, w), BF) for w in wide],
            *[v((128, w), F32) for w in wide],
            v((2, 32, CPAD), F32), v((4, 64, GRAM), BF),
            v((2, 4, 32, 128), F32), v((2, 4, 32, 128), F32), v((128, 128), F32), v((FRAMES, 128), F32),
            pltpu.SemaphoreType.DMA((SENDS,)), pltpu.SemaphoreType.DMA((RECVS,)), pltpu.SemaphoreType.DMA((6,)),
        ],
        compiler_params=pltpu.CompilerParams(collective_id=0, has_side_effects=True, vmem_limit_bytes=38 * 2**20),
        name="panels",
    )(inputs, projection, offsets.reshape(1, FEATS), labels, weights.T)
    new, loss = pl.pallas_call(
        last_kernel,
        grid=(TILES,),
        out_shape=(jax.ShapeDtypeStruct((CLS, FEATS), F32), jax.ShapeDtypeStruct((2,), F32)),
        in_specs=[vm, vm, vm, vm],
        out_specs=(
            pl.BlockSpec((128, FEATS), lambda i: (i, 0)),
            pl.BlockSpec(memory_space=pltpu.SMEM),
        ),
        compiler_params=pltpu.CompilerParams(vmem_limit_bytes=12 * 2**20),
        name="last_update",
    )(*kept)
    return new.T, loss


def solution(mesh):
    return jax.shard_map(
        per_device,
        mesh=mesh,
        in_specs=(P(None, "feat", None), P(None, "feat"), P("feat"), P(), P("feat", "cls")),
        out_specs=(P("feat", "cls"), P()),
        check_vma=False,
    )
```
